128 devices in a mesh: bead: 16 (over x, y_hi, core), atom: 8 (over z, y_lo).
Axes of the slice: x: 4, y: 4 (y_hi: 2, y_lo: 2; y = y_hi * 2 + y_lo), z: 4, core: 2. Of those that a mesh axis runs over, the one named last changes fastest.
Arguments:
- replica_point_fractions: float32 [128, 3, 12288], P('bead', None, 'atom'), may hold values from -1 to 2, as said below
- inverse_lattice_integers: int32 [3, 2048], P(None, 'bead'), may hold values from -10 to 10, as said below
- point_species_labels: int32 [12288], P('atom'), may hold values from 0 to 3
- species_electric_values: float32 [4], replicated, may hold values from -1 to 1
Outputs:
- bead_forces: float32 [128, 3, 12288], P('bead', None, 'atom')
The draws below stay inside these ranges and needn't reach their ends.
Inputs may be any that keep to these rules, and one draw needn't show every extreme that they name: replica_point_fractions holds a site's position near a common centre in all beads, with its own offset in each bead. `inverse_lattice_integers`: its columns are distinct, none is all zeros, and none is the negative of another (the first nonzero entry of each column is positive).
All inputs are finite; a program needn't handle non-finite values.
Results may differ from the reference program's by a relative error of at most 0.0003.
Values sent between devices are 32-bit elements; how exact they have to be, the bound alone decides.
No kernel may reach another device: no remote copies, remote signals or barrier semaphores. Data moves between devices by JAX's collectives and lax.ppermute only.
A program may use at most 64 MiB of HBM per device.

```python
import math
import jax
import jax.numpy as jnp
from jax import lax

BEADS = 128
CONTR = 8
KVEC = 2048
KINDS = 4
NSITES = 12288


def draw_replica_point_fractions(key, part):
    centre_key = jax.random.fold_in(key, 11)
    offset_key = jax.random.fold_in(key, 12)
    centre = jax.random.uniform(centre_key, (1, 3, NSITES), jnp.float32, 0.0, 1.0)
    offset = 0.08 * jax.random.normal(offset_key, (BEADS, 3, NSITES), jnp.float32)
    return (centre + offset).astype(jnp.float32)


def draw_inverse_lattice_integers(key, part):
    side = 21
    total = side * side * side
    index = jnp.arange(total, dtype=jnp.int32)
    first = index // (side * side) - 10
    second = index // side % side - 10
    third = index % side - 10
    upper = (first > 0) | (first == 0) & (second > 0) | (first == 0) & (second == 0) & (third > 0)
    order = jax.random.permutation(jax.random.fold_in(key, 21), total).astype(jnp.int32)
    rank = jnp.zeros((total,), jnp.int32).at[order].set(index)
    score = jnp.where(upper, rank, rank + total)
    chosen = jnp.argsort(score, stable=True)[:KVEC]
    return jnp.stack([first[chosen], second[chosen], third[chosen]]).astype(jnp.int32)


def set_ends(drawn, stream_key, low, largest):
    place = [jax.random.randint(jax.random.fold_in(stream_key, axis), (), 0, length) for axis, length in enumerate(drawn.shape)]
    main_axis = drawn.shape.index(max(drawn.shape))
    next_to = place[:main_axis] + [(place[main_axis] + 1) % drawn.shape[main_axis]] + place[main_axis + 1:]
    return drawn.at[tuple(place)].set(low).at[tuple(next_to)].set(largest)


def setup_inputs(seed: int = 0) -> dict:
    splits = jax.random.split(jax.random.key(seed), 5)
    replica_point_fractions = draw_replica_point_fractions(jax.random.fold_in(splits[4], 71), 0)
    inverse_lattice_integers = draw_inverse_lattice_integers(jax.random.fold_in(splits[4], 71), 0)
    point_species_labels = set_ends(jax.random.randint(splits[2], (NSITES,), 0, KINDS), jax.random.fold_in(splits[2], 1), 0, KINDS - 1).astype(jnp.int32)
    species_electric_values = jnp.clip(jax.random.uniform(splits[3], (KINDS,), jnp.float32, -1.0, 1.0), -1.0, 1.0)
    return dict(replica_point_fractions=replica_point_fractions, inverse_lattice_integers=inverse_lattice_integers, point_species_labels=point_species_labels, species_electric_values=species_electric_values)


TWO_PI = 2.0 * math.pi

def cycle_modes(length, count):
    index = jnp.arange(length, dtype=jnp.float32)
    rows = [jnp.ones((length,), jnp.float32) / math.sqrt(length)]
    for mode in range(1, count // 2):
        rows.append(math.sqrt(2.0 / length) * jnp.cos(TWO_PI * mode * index / length))
        rows.append(math.sqrt(2.0 / length) * jnp.sin(TWO_PI * mode * index / length))
    if length == count:
        rows.append(jnp.cos(math.pi * index) / math.sqrt(length))
    else:
        rows.append(math.sqrt(2.0 / length) * jnp.cos(TWO_PI * (count // 2) * index / length))
    return jnp.stack(rows)

def contraction_table(beads, contr):
    small = cycle_modes(contr, contr)
    big = cycle_modes(beads, contr)
    return math.sqrt(contr / beads) * jnp.dot(small.T, big, precision=lax.Precision.HIGHEST)

def reference(replica_point_fractions, inverse_lattice_integers, point_species_labels, species_electric_values):
    table = contraction_table(BEADS, CONTR)
    contracted = jnp.einsum('jb,bxs->jxs', table, replica_point_fractions, precision=lax.Precision.HIGHEST)
    kinds = jnp.arange(species_electric_values.shape[0], dtype=jnp.int32)
    charge = lax.optimization_barrier(jnp.sum((point_species_labels[None, :] == kinds[:, None]).astype(jnp.float32) * species_electric_values[:, None], axis=0))
    fourier_mode_table = inverse_lattice_integers.astype(jnp.float32)
    square = lax.optimization_barrier(jnp.sum(fourier_mode_table * fourier_mode_table, axis=0))
    fourier_mode_factor = 4.0 * jnp.exp(-square / 100.0) / (square * NSITES)
    block = min(256, KVEC)
    nblocks = KVEC // block
    wave_blocks = jnp.transpose(fourier_mode_table.reshape(3, nblocks, block), (1, 0, 2))
    weight_blocks = fourier_mode_factor.reshape(nblocks, block)

    def per_bead(position):

        def factor_block(wave):
            angle = TWO_PI * jnp.dot(wave.T, position, precision=lax.Precision.HIGHEST)
            return (jnp.dot(jnp.cos(angle), charge, precision=lax.Precision.HIGHEST), jnp.dot(jnp.sin(angle), charge, precision=lax.Precision.HIGHEST))
        cos_fac, sin_fac = lax.map(factor_block, wave_blocks)

        def force_block(total, items):
            wave, wgt, cfac, sfac = items
            angle = TWO_PI * jnp.dot(wave.T, position, precision=lax.Precision.HIGHEST)
            left = TWO_PI * wave * (wgt * cfac)[None, :]
            right = TWO_PI * wave * (wgt * sfac)[None, :]
            term = jnp.dot(left, jnp.sin(angle), precision=lax.Precision.HIGHEST) - jnp.dot(right, jnp.cos(angle), precision=lax.Precision.HIGHEST)
            return (total + term, None)
        start = jnp.zeros((3, position.shape[1]), jnp.float32)
        total, unused = lax.scan(force_block, start, (wave_blocks, weight_blocks, cos_fac, sin_fac))
        return charge[None, :] * total
    force = lax.map(per_bead, contracted)
    return jnp.einsum('jb,jxs->bxs', table, force, precision=lax.Precision.HIGHEST)
```

```python
import functools
import math

import jax
import jax.numpy as jnp
import numpy as np
from jax import lax
from jax.experimental import pallas as pl
from jax.experimental.pallas import tpu as pltpu
from jax.sharding import PartitionSpec as P

CONTR = 8
TOP = 10
SIDE = 2 * TOP + 1
PAIRS = (TOP + 1) * SIDE
HALF = (PAIRS + 1) // 2
LANES = 128
ROWS = 16
SENT = 12
TWO_PI = 2.0 * math.pi


def polynomials():
    nodes = 0.5 * np.cos(np.pi * (np.arange(400) + 0.5) / 400)
    u = nodes * nodes
    odd = np.linalg.lstsq(
        nodes[:, None] * u[:, None] ** np.arange(7), np.sin(2 * np.pi * nodes), rcond=None
    )[0]
    even = np.linalg.lstsq(u[:, None] ** np.arange(8), np.cos(2 * np.pi * nodes), rcond=None)[0]
    return [float(c) for c in odd], [float(c) for c in even]


ODD, EVEN = polynomials()


def horner(u, coefficients):
    total = coefficients[-1]
    for c in coefficients[-2::-1]:
        total = total * u + c
    return total


def reduced(t):
    return t - jnp.round(t)


def sin_turns(t):
    t = reduced(t)
    return t * horner(t * t, ODD)


def both_turns(t):
    t = reduced(t)
    u = t * t
    return horner(u, EVEN), t * horner(u, ODD)


def cycle_modes(length, count):
    index = np.arange(length, dtype=np.float64)
    rows = [np.ones(length) / math.sqrt(length)]
    for mode in range(1, count // 2):
        rows.append(math.sqrt(2.0 / length) * np.cos(TWO_PI * mode * index / length))
        rows.append(math.sqrt(2.0 / length) * np.sin(TWO_PI * mode * index / length))
    if length == count:
        rows.append(np.cos(math.pi * index) / math.sqrt(length))
    else:
        rows.append(math.sqrt(2.0 / length) * np.cos(TWO_PI * (count // 2) * index / length))
    return np.stack(rows)


def contraction_table(beads, contr):
    small = cycle_modes(contr, contr)
    big = cycle_modes(beads, contr)
    return (math.sqrt(contr / beads) * small.T @ big).astype(np.float32)


def iota(shape, dim):
    return lax.broadcasted_iota(jnp.int32, shape, dim).astype(jnp.float32)


def pair_of(index):
    m2 = jnp.floor((index + 0.5) * (1.0 / SIDE))
    return m2, index - m2 * SIDE - TOP


def split(value):
    high = value.astype(jnp.bfloat16)
    low = (value - high.astype(jnp.float32)).astype(jnp.bfloat16)
    return high, low


def dot_nt(a, b):
    return lax.dot_general(a, b, (((1,), (1,)), ((), ())), preferred_element_type=jnp.float32)


def contract_kernel(table_ref, points_ref, waves_ref, out_ref, work_ref):
    beads = points_ref.shape[1]
    tiles = points_ref.shape[2] // LANES
    columns = [
        jnp.broadcast_to(table_ref[:, b : b + 1], (CONTR, LANES)) for b in range(beads)
    ]
    for x in range(3):
        for t in range(tiles):
            block = points_ref[x, :, t * LANES : (t + 1) * LANES]
            total = columns[0] * jnp.broadcast_to(block[0:1], (CONTR, LANES))
            for b in range(1, beads):
                total += columns[b] * jnp.broadcast_to(block[b : b + 1], (CONTR, LANES))
            row = (x * tiles + t) * CONTR
            work_ref[row : row + CONTR, :] = total
    waves = waves_ref[...].astype(jnp.float32)
    used = 3 * tiles
    copies = out_ref.shape[0] // CONTR
    for j in range(CONTR):
        rows = work_ref[pl.ds(j, used, stride=CONTR), :]
        for c in range(copies):
            out_ref[j * copies + c, 0:used, :] = rows
            out_ref[j * copies + c, used : used + 3, :] = waves


def structure_kernel(
    number_points,
    spots_ref,
    labels_ref,
    species_ref,
    partial_ref,
    weights_ref,
    high_ref,
    low_ref,
    plain_ref,
    slope_ref,
    charged_ref,
):
    core = lax.rem(lax.axis_index("bead"), 2).astype(jnp.float32)
    peers = spots_ref.shape[0]
    tiles = labels_ref.shape[0]
    used = 3 * tiles
    spots = spots_ref[0, 0:used, :]
    for p in range(1, peers):
        spots += spots_ref[p, 0:used, :]
    spots = reduced(spots)
    labels = labels_ref[...]
    charge = jnp.zeros(labels.shape, jnp.float32)
    for kind in range(species_ref.shape[0]):
        charge += jnp.where(labels == kind, species_ref[kind], 0.0)
    first = core * HALF
    grid_row = iota((2 * ROWS, LANES), 0)
    back = grid_row >= ROWS
    size = jnp.where(back, grid_row - ROWS, grid_row)
    wanted = jnp.where(back, jnp.where(size > 0, -size, 1000.0), size)
    pair_row = iota((LANES, LANES), 0)
    counts = jnp.zeros((2 * ROWS, LANES), jnp.float32)
    for p in range(peers):
        m1 = spots_ref[p, used : used + 1, :]
        m2 = spots_ref[p, used + 1 : used + 2, :]
        m3 = spots_ref[p, used + 2 : used + 3, :]
        sign = jnp.where(m2 < 0, -1.0, 1.0)
        place = (m2 * sign) * SIDE + (m3 * sign) + TOP - first
        place = jnp.where(place < HALF, place, -1.0)
        left = jnp.where(wanted == m1 * sign, 1.0, 0.0).astype(jnp.bfloat16)
        right = jnp.where(pair_row == place, 1.0, 0.0).astype(jnp.bfloat16)
        counts += dot_nt(left, right)
    m2, m3 = pair_of(iota((2 * ROWS, LANES), 1) + first)
    square = size * size + m2 * m2 + m3 * m3
    square = jnp.maximum(square, 1.0)
    weights_ref[...] = counts * (4.0 * jnp.exp(square * -0.01) / (square * number_points))
    row = iota((2 * ROWS, LANES), 0)
    sine = row >= ROWS
    m1 = jnp.where(sine, row - ROWS, row)
    phase = jnp.where(sine, 0.0, 0.25)
    chunk = 32
    for t in range(tiles):
        lanes = slice(t * LANES, (t + 1) * LANES)
        x1 = spots[t : t + 1, :]
        q = charge[t : t + 1, :]
        angle = m1 * x1 + phase
        plain = q * sin_turns(angle)
        plain_ref[:, lanes] = plain
        slope_ref[:, lanes] = (q * (-TWO_PI)) * m1 * sin_turns(angle + 0.25)
        high, low = split(plain)
        charged_ref[0 : 2 * ROWS, lanes] = high
        charged_ref[2 * ROWS :, lanes] = low
    for r in range(0, LANES, chunk):
        m2, m3 = pair_of(iota((chunk, LANES), 0) + (first + r))
        for t in range(tiles):
            lanes = slice(t * LANES, (t + 1) * LANES)
            x2 = spots[tiles + t : tiles + t + 1, :]
            x3 = spots[2 * tiles + t : 2 * tiles + t + 1, :]
            cosine, sine = both_turns(m2 * x2 + m3 * x3)
            high, low = split(cosine)
            high_ref[r : r + chunk, lanes] = high
            low_ref[r : r + chunk, lanes] = low
            high, low = split(sine)
            high_ref[LANES + r : LANES + r + chunk, lanes] = high
            low_ref[LANES + r : LANES + r + chunk, lanes] = low
    total = dot_nt(charged_ref[...], high_ref[...])
    total = (
        total[0 : 2 * ROWS]
        + total[2 * ROWS :]
        + dot_nt(charged_ref[0 : 2 * ROWS, :], low_ref[...])
    )
    for p in range(partial_ref.shape[0]):
        partial_ref[p, 0:SENT, :] = total[0:SENT]
        partial_ref[p, SENT:, :] = total[ROWS : ROWS + SENT]


def force_kernel(
    partial_ref, weights_ref, high_ref, low_ref, plain_ref, slope_ref, out_ref, coef_ref, term_ref
):
    core = lax.rem(lax.axis_index("bead"), 2).astype(jnp.float32)
    tiles = plain_ref.shape[1] // LANES
    cos_row = partial_ref[0, 0:SENT, :]
    sin_row = partial_ref[0, SENT:, :]
    for p in range(1, partial_ref.shape[0]):
        cos_row += partial_ref[p, 0:SENT, :]
        sin_row += partial_ref[p, SENT:, :]
    ahead = weights_ref[0:SENT, :]
    back = weights_ref[ROWS : ROWS + SENT, :]
    cc, cs = cos_row[:, :LANES], cos_row[:, LANES:]
    sc, ss = sin_row[:, :LANES], sin_row[:, LANES:]
    ahead_cos, ahead_sin = ahead * (cc - ss), ahead * (cs + sc)
    back_cos, back_sin = back * (cc + ss), back * (cs - sc)
    m2, m3 = pair_of(iota((SENT, LANES), 1) + core * HALF)
    coef_ref[...] = jnp.zeros_like(coef_ref)
    rows = (
        (ahead_cos + back_cos, ahead_sin + back_sin),
        (ahead_sin - back_sin, back_cos - ahead_cos),
    )
    for kind, (on_cos, on_sin) in enumerate(rows):
        at = kind * ROWS
        coef_ref[at : at + SENT, :LANES] = on_cos
        coef_ref[at : at + SENT, LANES:] = on_sin
        for axis, m in enumerate((m2, m3)):
            at = kind * ROWS + 2 * ROWS * (axis + 1)
            coef_ref[at : at + SENT, :LANES] = (-TWO_PI) * m * on_sin
            coef_ref[at : at + SENT, LANES:] = TWO_PI * m * on_cos
    high, low = split(coef_ref[...])
    both = jnp.concatenate([high, low], axis=0)
    size = high.shape[0]
    width = 2 * LANES
    for t in range(0, tiles, 2):
        lanes = slice(t * LANES, t * LANES + width)
        near = jnp.dot(both, high_ref[:, lanes], preferred_element_type=jnp.float32)
        far = jnp.dot(high, low_ref[:, lanes], preferred_element_type=jnp.float32)
        term = near[:size] + near[size:] + far
        plain = plain_ref[:, lanes]
        values = [term[0 : 2 * ROWS] * slope_ref[:, lanes]]
        for axis in range(2):
            at = 2 * ROWS * (axis + 1)
            values.append(term[at : at + 2 * ROWS] * plain)
        for x, value in enumerate(values):
            total = jnp.sum(value, axis=0, keepdims=True)
            for i in range(2):
                term_ref[x * tiles + t + i : x * tiles + t + i + 1, :] = total[
                    :, i * LANES : (i + 1) * LANES
                ]
    block = term_ref[...]
    for p in range(out_ref.shape[0]):
        out_ref[p, 0 : block.shape[0], :] = block


def expand_kernel(table_ref, force_ref, out_ref, work_ref):
    beads = out_ref.shape[1]
    tiles = out_ref.shape[2] // LANES
    used = 3 * tiles
    stride = work_ref.shape[0] // beads
    copies = force_ref.shape[0] // CONTR
    parts = []
    for j in range(CONTR):
        part = force_ref[j * copies, 0:used, :]
        for c in range(1, copies):
            part += force_ref[j * copies + c, 0:used, :]
        parts.append(part)
    for b in range(beads):
        total = parts[0] * table_ref[b, 0]
        for j in range(1, CONTR):
            total += parts[j] * table_ref[b, j]
        work_ref[b * stride : b * stride + used, :] = total
    for x in range(3):
        for t in range(tiles):
            out_ref[x, :, t * LANES : (t + 1) * LANES] = work_ref[
                pl.ds(x * tiles + t, beads, stride=stride), :
            ]


VMEM = pl.BlockSpec(memory_space=pltpu.VMEM)
SMEM = pl.BlockSpec(memory_space=pltpu.SMEM)
PARAMS = pltpu.CompilerParams(vmem_limit_bytes=24 * 1024 * 1024)


def shaped(*shape, dtype=jnp.float32):
    return jax.ShapeDtypeStruct(shape, dtype)


def local(points, waves, labels, species):
    beads, _, sites = points.shape
    bead_peers = lax.axis_size("bead")
    atom_peers = lax.axis_size("atom")
    tiles = sites // LANES
    used = 3 * tiles
    sent = -(-(used + 3) // 8) * 8
    held = -(-used // 8) * 8
    table = contraction_table(beads * bead_peers, CONTR)
    blocks = jnp.asarray(table.reshape(CONTR, bead_peers, beads).transpose(1, 0, 2))
    mine = lax.dynamic_index_in_dim(blocks, lax.axis_index("bead"), 0, keepdims=False)
    portion = pl.pallas_call(
        contract_kernel,
        out_shape=shaped(bead_peers, sent, LANES),
        in_specs=[VMEM] * 3,
        out_specs=VMEM,
        scratch_shapes=[pltpu.VMEM((used * CONTR, LANES), jnp.float32)],
        compiler_params=PARAMS,
        name="contract",
    )(mine, points.transpose(1, 0, 2), waves)
    spots = lax.all_to_all(portion, "bead", 0, 0, tiled=True)
    partial, weights, high, low, plain, slope = pl.pallas_call(
        functools.partial(structure_kernel, float(sites * atom_peers)),
        out_shape=[
            shaped(atom_peers, 2 * SENT, 2 * LANES),
            shaped(2 * ROWS, LANES),
            shaped(2 * LANES, sites, dtype=jnp.bfloat16),
            shaped(2 * LANES, sites, dtype=jnp.bfloat16),
            shaped(2 * ROWS, sites),
            shaped(2 * ROWS, sites),
        ],
        in_specs=[VMEM, VMEM, SMEM],
        out_specs=[VMEM] * 6,
        scratch_shapes=[pltpu.VMEM((4 * ROWS, sites), jnp.bfloat16)],
        compiler_params=PARAMS,
        name="structure",
    )(spots, labels.reshape(tiles, LANES), species)
    factors = lax.all_to_all(partial, "atom", 0, 0, tiled=True)
    force = pl.pallas_call(
        force_kernel,
        out_shape=shaped(bead_peers, held, LANES),
        in_specs=[VMEM] * 6,
        out_specs=VMEM,
        scratch_shapes=[
            pltpu.VMEM((6 * ROWS, 2 * LANES), jnp.float32),
            pltpu.VMEM((used, LANES), jnp.float32),
        ],
        compiler_params=PARAMS,
        name="force",
    )(factors, weights, high, low, plain, slope)
    forces = lax.all_to_all(force, "bead", 0, 0, tiled=True)
    out = pl.pallas_call(
        expand_kernel,
        out_shape=shaped(3, beads, sites),
        in_specs=[SMEM, VMEM],
        out_specs=VMEM,
        scratch_shapes=[pltpu.VMEM((beads * held, LANES), jnp.float32)],
        compiler_params=PARAMS,
        name="expand",
    )(mine.T, forces)
    return out.transpose(1, 0, 2)


def solution(mesh):
    in_specs = (P("bead", None, "atom"), P(None, "bead"), P("atom"), P())
    out_specs = P("bead", None, "atom")
    return jax.shard_map(local, mesh=mesh, in_specs=in_specs, out_specs=out_specs, check_vma=False)
```

```python
import functools
import math

import jax
import jax.numpy as jnp
import numpy as np
from jax import lax
from jax.experimental import pallas as pl
from jax.experimental.pallas import tpu as pltpu
from jax.sharding import PartitionSpec as P

CONTR = 8
LANES = 128
ROWS = 16
SENT = 12
TWO_PI = 2.0 * math.pi


def polynomials():
    nodes = 0.5 * np.cos(np.pi * (np.arange(400) + 0.5) / 400)
    u = nodes * nodes
    odd = np.linalg.lstsq(
        nodes[:, None] * u[:, None] ** np.arange(7), np.sin(2 * np.pi * nodes), rcond=None
    )[0]
    even = np.linalg.lstsq(u[:, None] ** np.arange(8), np.cos(2 * np.pi * nodes), rcond=None)[0]
    return [float(c) for c in odd], [float(c) for c in even]


ODD, EVEN = polynomials()


def horner(u, coefficients):
    total = coefficients[-1]
    for c in coefficients[-2::-1]:
        total = total * u + c
    return total


def reduced(t):
    return t - jnp.round(t)


def sin_turns(t):
    t = reduced(t)
    return t * horner(t * t, ODD)


def cos_turns(t):
    t = reduced(t)
    return horner(t * t, EVEN)


def both_turns(t):
    t = reduced(t)
    u = t * t
    return horner(u, EVEN), t * horner(u, ODD)


def iota(shape, dim):
    return lax.broadcasted_iota(jnp.int32, shape, dim).astype(jnp.float32)


def pair_of(index, core):
    tile = jnp.floor(index * 0.125)
    place = index - 8.0 * tile
    run = jnp.floor((tile + 0.5) * 0.2)
    m2 = tile - 5.0 * run + 1.0 + 5.0 * core
    last = run > 2.5
    m2 = jnp.where(last, 0.0, m2)
    run = jnp.where(last, core, run)
    return m2, run_member(run, place)


def run_member(run, place):
    middle = jnp.where(place < 3, place + 8.0, -6.0 - place)
    return jnp.where(run < 0.5, place, jnp.where(run < 1.5, middle, -1.0 - place))


def place_of(m2, m3, core):
    size = jnp.abs(m3)
    outer = size > 8.5
    middle = outer | (m3 == 8.0)
    run = jnp.where(middle, 1.0, jnp.where(m3 < 0, 2.0, 0.0))
    place = jnp.where(middle, jnp.where(m3 < 0, size - 6.0, m3 - 8.0), jnp.where(m3 < 0, size - 1.0, m3))
    step = m2 - 1.0 - 5.0 * core
    row = (run * 5.0 + step) * 8.0 + place
    row = jnp.where((step >= 0) & (step < 5), row, -1.0)
    return jnp.where(m2 == 0.0, jnp.where(run == core, 120.0 + place, -1.0), row)


def split(value):
    high = value.astype(jnp.bfloat16)
    low = (value - high.astype(jnp.float32)).astype(jnp.bfloat16)
    return high, low


def dot_nt(a, b):
    return lax.dot_general(a, b, (((1,), (1,)), ((), ())), preferred_element_type=jnp.float32)


def table_value(bead, contracted, beads):
    turn = bead * (1.0 / beads) - contracted * (1.0 / CONTR)
    total = 1.0 + math.sqrt(2.0) * cos_turns(turn * (CONTR // 2))
    for mode in range(1, CONTR // 2):
        total += 2.0 * cos_turns(turn * mode)
    return total * (1.0 / beads)


def contract_kernel(
    beads_all,
    points_from,
    waves_from,
    labels_from,
    species_from,
    out_ref,
    charge_ref,
    work_ref,
    points_ref,
    waves_ref,
    labels_ref,
    species_ref,
    sems,
):
    copies_in = [
        pltpu.make_async_copy(points_from.at[x], points_ref.at[x], sems.at[x]) for x in range(3)
    ]
    for i, (source, target) in enumerate(
        ((waves_from, waves_ref), (labels_from, labels_ref), (species_from, species_ref))
    ):
        copies_in.append(pltpu.make_async_copy(source, target, sems.at[3 + i]))
    for copy in copies_in:
        copy.start()
    beads = points_ref.shape[1]
    tiles = points_ref.shape[2] // LANES
    first = (lax.axis_index("bead") * beads).astype(jnp.float32)
    columns = [
        table_value(first + b, iota((CONTR, LANES), 0), beads_all) for b in range(beads)
    ]
    for x in range(3):
        copies_in[x].wait()
        for t in range(tiles):
            block = points_ref[x, :, t * LANES : (t + 1) * LANES]
            total = columns[0] * jnp.broadcast_to(block[0:1], (CONTR, LANES))
            for b in range(1, beads):
                total += columns[b] * jnp.broadcast_to(block[b : b + 1], (CONTR, LANES))
            row = (x * tiles + t) * CONTR
            work_ref[row : row + CONTR, :] = total
    for copy in copies_in[3:]:
        copy.wait()
    waves = waves_ref[...].astype(jnp.float32)
    used = 3 * tiles
    copies = out_ref.shape[0] // CONTR
    for j in range(CONTR):
        rows = work_ref[pl.ds(j, used, stride=CONTR), :]
        for c in range(copies):
            out_ref[j * copies + c, 0:used, :] = rows
            out_ref[j * copies + c, used : used + 3, :] = waves
    labels = labels_ref[...]
    charge = jnp.zeros(labels.shape, jnp.float32)
    for kind in range(species_ref.shape[1]):
        value = jnp.broadcast_to(species_ref[:, kind : kind + 1], labels.shape)
        charge += jnp.where(labels == kind, value, 0.0)
    charge_ref[...] = charge


def structure_kernel(
    number_points,
    spots_ref,
    charge_ref,
    partial_ref,
    weights_ref,
    high_ref,
    low_ref,
    plain_ref,
    slope_ref,
    charged_ref,
):
    core = lax.rem(lax.axis_index("bead"), 2).astype(jnp.float32)
    peers = spots_ref.shape[0]
    tiles = charge_ref.shape[0]
    used = 3 * tiles
    spots = spots_ref[0, 0:used, :]
    for p in range(1, peers):
        spots += spots_ref[p, 0:used, :]
    spots = reduced(spots)
    charge = charge_ref[...]
    grid_row = iota((2 * ROWS, LANES), 0)
    back = grid_row >= ROWS
    size = jnp.where(back, grid_row - ROWS, grid_row)
    wanted = jnp.where(back, jnp.where(size > 0, -size, 1000.0), size)
    pair_row = iota((LANES, LANES), 0)
    counts = jnp.zeros((2 * ROWS, LANES), jnp.float32)
    for p in range(peers):
        m1 = spots_ref[p, used : used + 1, :]
        m2 = spots_ref[p, used + 1 : used + 2, :]
        m3 = spots_ref[p, used + 2 : used + 3, :]
        sign = jnp.where(m2 < 0, -1.0, 1.0)
        fold = m2 * sign
        m3 = m3 * sign
        flip = jnp.where((fold == 0) & (m3 < 0), -1.0, 1.0)
        sign = sign * flip
        place = place_of(fold, m3 * flip, core)
        left = jnp.where(wanted == m1 * sign, 1.0, 0.0).astype(jnp.bfloat16)
        right = jnp.where(pair_row == place, 1.0, 0.0).astype(jnp.bfloat16)
        counts += dot_nt(left, right)
    m2, m3 = pair_of(iota((2 * ROWS, LANES), 1), core)
    square = size * size + m2 * m2 + m3 * m3
    square = jnp.maximum(square, 1.0)
    weights_ref[...] = counts * (4.0 * jnp.exp(square * -0.01) / (square * number_points))
    row = iota((2 * ROWS, LANES), 0)
    sine = row >= ROWS
    m1 = jnp.where(sine, row - ROWS, row)
    phase = jnp.where(sine, 0.0, 0.25)
    for t in range(tiles):
        lanes = slice(t * LANES, (t + 1) * LANES)
        x1 = spots[t : t + 1, :]
        q = charge[t : t + 1, :]
        angle = m1 * x1 + phase
        plain = q * sin_turns(angle)
        plain_ref[:, lanes] = plain
        slope_ref[:, lanes] = (q * (-TWO_PI)) * m1 * sin_turns(angle + 0.25)
        high, low = split(plain)
        charged_ref[0 : 2 * ROWS, lanes] = high
        charged_ref[2 * ROWS :, lanes] = low
    steps = 1.0 + 5.0 * core + iota((8, LANES), 0)
    runs = [run_member(jnp.full((8, LANES), float(run)), iota((8, LANES), 0)) for run in range(3)]
    for t in range(tiles):
        lanes = slice(t * LANES, (t + 1) * LANES)
        x2 = spots[tiles + t : tiles + t + 1, :]
        x3 = spots[2 * tiles + t : 2 * tiles + t + 1, :]
        cos2, sin2 = both_turns(steps * x2)
        third = [both_turns(m * x3) for m in runs]
        cosines, sines = [], []
        for run in range(3):
            cos3, sin3 = third[run]
            for i in range(5):
                c2 = jnp.broadcast_to(cos2[i : i + 1], (8, LANES))
                s2 = jnp.broadcast_to(sin2[i : i + 1], (8, LANES))
                cosines.append(c2 * cos3 - s2 * sin3)
                sines.append(s2 * cos3 + c2 * sin3)
        for values, index in ((cosines, 0), (sines, 1)):
            values.append(jnp.where(core == 0.0, third[0][index], third[1][index]))
            for r in range(0, 16, 2):
                high, low = split(jnp.concatenate(values[r : r + 2], axis=0))
                at = index * LANES + r * 8
                high_ref[at : at + 16, lanes] = high
                low_ref[at : at + 16, lanes] = low
    total = dot_nt(charged_ref[...], high_ref[...])
    total = (
        total[0 : 2 * ROWS]
        + total[2 * ROWS :]
        + dot_nt(charged_ref[0 : 2 * ROWS, :], low_ref[...])
    )
    for p in range(partial_ref.shape[0]):
        partial_ref[p, 0:SENT, :] = total[0:SENT]
        partial_ref[p, SENT:, :] = total[ROWS : ROWS + SENT]


def force_kernel(
    partial_ref, weights_ref, high_ref, low_ref, plain_ref, slope_ref, out_ref, coef_ref, term_ref
):
    core = lax.rem(lax.axis_index("bead"), 2).astype(jnp.float32)
    tiles = plain_ref.shape[1] // LANES
    cos_row = partial_ref[0, 0:SENT, :]
    sin_row = partial_ref[0, SENT:, :]
    for p in range(1, partial_ref.shape[0]):
        cos_row += partial_ref[p, 0:SENT, :]
        sin_row += partial_ref[p, SENT:, :]
    ahead = weights_ref[0:SENT, :]
    back = weights_ref[ROWS : ROWS + SENT, :]
    cc, cs = cos_row[:, :LANES], cos_row[:, LANES:]
    sc, ss = sin_row[:, :LANES], sin_row[:, LANES:]
    ahead_cos, ahead_sin = ahead * (cc - ss), ahead * (cs + sc)
    back_cos, back_sin = back * (cc + ss), back * (cs - sc)
    m2, m3 = pair_of(iota((SENT, LANES), 1), core)
    coef_ref[...] = jnp.zeros_like(coef_ref)
    rows = (
        (ahead_cos + back_cos, ahead_sin + back_sin),
        (ahead_sin - back_sin, back_cos - ahead_cos),
    )
    for kind, (on_cos, on_sin) in enumerate(rows):
        at = kind * ROWS
        coef_ref[at : at + SENT, :LANES] = on_cos
        coef_ref[at : at + SENT, LANES:] = on_sin
        for axis, m in enumerate((m2, m3)):
            at = kind * ROWS + 2 * ROWS * (axis + 1)
            coef_ref[at : at + SENT, :LANES] = (-TWO_PI) * m * on_sin
            coef_ref[at : at + SENT, LANES:] = TWO_PI * m * on_cos
    high, low = split(coef_ref[...])
    both = jnp.concatenate([high, low], axis=0)
    size = high.shape[0]
    width = 2 * LANES
    for t in range(0, tiles, 2):
        lanes = slice(t * LANES, t * LANES + width)
        near = jnp.dot(both, high_ref[:, lanes], preferred_element_type=jnp.float32)
        far = jnp.dot(high, low_ref[:, lanes], preferred_element_type=jnp.float32)
        term = near[:size] + near[size:] + far
        plain = plain_ref[:, lanes]
        values = [term[0 : 2 * ROWS] * slope_ref[:, lanes]]
        for axis in range(2):
            at = 2 * ROWS * (axis + 1)
            values.append(term[at : at + 2 * ROWS] * plain)
        for x, value in enumerate(values):
            total = jnp.sum(value, axis=0, keepdims=True)
            for i in range(2):
                term_ref[x * tiles + t + i : x * tiles + t + i + 1, :] = total[
                    :, i * LANES : (i + 1) * LANES
                ]
    block = term_ref[...]
    for p in range(out_ref.shape[0]):
        out_ref[p, 0 : block.shape[0], :] = block


def expand_kernel(beads_all, force_ref, out_to, work_ref, out_ref, sems):
    beads = out_ref.shape[1]
    tiles = out_ref.shape[2] // LANES
    used = 3 * tiles
    stride = work_ref.shape[0] // beads
    copies = force_ref.shape[0] // CONTR
    first = (lax.axis_index("bead") * beads).astype(jnp.float32)
    rows = iota((beads * CONTR, LANES), 0)
    bead = jnp.floor((rows + 0.5) * (1.0 / CONTR))
    table = table_value(first + bead, rows - CONTR * bead, beads_all)
    done = 0
    moves = []
    for r in range(0, used, 8):
        size = min(8, used - r)
        parts = []
        for j in range(CONTR):
            part = force_ref[j * copies, r : r + size, :]
            for c in range(1, copies):
                part += force_ref[j * copies + c, r : r + size, :]
            parts.append(part)
        for b in range(beads):
            at = b * CONTR
            total = parts[0] * table[at : at + 1]
            for j in range(1, CONTR):
                total += parts[j] * table[at + j : at + j + 1]
            work_ref[b * stride + r : b * stride + r + size, :] = total
        for i in range(r, r + size):
            x, t = divmod(i, tiles)
            out_ref[x, :, t * LANES : (t + 1) * LANES] = work_ref[
                pl.ds(i, beads, stride=stride), :
            ]
        while done < 3 and (done + 1) * tiles <= r + size:
            moves.append(pltpu.make_async_copy(out_ref.at[done], out_to.at[done], sems.at[done]))
            moves[-1].start()
            done += 1
    for move in moves:
        move.wait()


VMEM = pl.BlockSpec(memory_space=pltpu.VMEM)
HBM = pl.BlockSpec(memory_space=pltpu.HBM)
PARAMS = pltpu.CompilerParams(vmem_limit_bytes=24 * 1024 * 1024)


def shaped(*shape, dtype=jnp.float32):
    return jax.ShapeDtypeStruct(shape, dtype)


def local(points, waves, labels, species):
    beads, _, sites = points.shape
    bead_peers = lax.axis_size("bead")
    atom_peers = lax.axis_size("atom")
    tiles = sites // LANES
    used = 3 * tiles
    sent = -(-(used + 3) // 8) * 8
    held = -(-used // 8) * 8
    beads_all = beads * bead_peers
    portion, charge = pl.pallas_call(
        functools.partial(contract_kernel, beads_all),
        out_shape=[shaped(bead_peers, sent, LANES), shaped(tiles, LANES)],
        in_specs=[HBM] * 4,
        out_specs=[VMEM] * 2,
        scratch_shapes=[
            pltpu.VMEM((used * CONTR, LANES), jnp.float32),
            pltpu.VMEM((3, beads, sites), jnp.float32),
            pltpu.VMEM(waves.shape, jnp.int32),
            pltpu.VMEM((tiles, LANES), jnp.int32),
            pltpu.VMEM((1, species.shape[0]), jnp.float32),
            pltpu.SemaphoreType.DMA((6,)),
        ],
        compiler_params=PARAMS,
        name="contract",
    )(
        *(
            pltpu.with_memory_space_constraint(a, pltpu.HBM)
            for a in (
                points.transpose(1, 0, 2),
                waves,
                labels.reshape(tiles, LANES),
                species[None, :],
            )
        )
    )
    spots = lax.all_to_all(portion, "bead", 0, 0, tiled=True)
    partial, weights, high, low, plain, slope = pl.pallas_call(
        functools.partial(structure_kernel, float(sites * atom_peers)),
        out_shape=[
            shaped(atom_peers, 2 * SENT, 2 * LANES),
            shaped(2 * ROWS, LANES),
            shaped(2 * LANES, sites, dtype=jnp.bfloat16),
            shaped(2 * LANES, sites, dtype=jnp.bfloat16),
            shaped(2 * ROWS, sites),
            shaped(2 * ROWS, sites),
        ],
        in_specs=[VMEM] * 2,
        out_specs=[VMEM] * 6,
        scratch_shapes=[pltpu.VMEM((4 * ROWS, sites), jnp.bfloat16)],
        compiler_params=PARAMS,
        name="structure",
    )(spots, charge)
    factors = lax.all_to_all(partial, "atom", 0, 0, tiled=True)
    force = pl.pallas_call(
        force_kernel,
        out_shape=shaped(bead_peers, held, LANES),
        in_specs=[VMEM] * 6,
        out_specs=VMEM,
        scratch_shapes=[
            pltpu.VMEM((6 * ROWS, 2 * LANES), jnp.float32),
            pltpu.VMEM((used, LANES), jnp.float32),
        ],
        compiler_params=PARAMS,
        name="force",
    )(factors, weights, high, low, plain, slope)
    forces = lax.all_to_all(force, "bead", 0, 0, tiled=True)
    out = pl.pallas_call(
        functools.partial(expand_kernel, beads_all),
        out_shape=shaped(3, beads, sites),
        in_specs=[VMEM],
        out_specs=HBM,
        scratch_shapes=[
            pltpu.VMEM((beads * held, LANES), jnp.float32),
            pltpu.VMEM((3, beads, sites), jnp.float32),
            pltpu.SemaphoreType.DMA((3,)),
        ],
        compiler_params=PARAMS,
        name="expand",
    )(forces)
    return out.transpose(1, 0, 2)


def solution(mesh):
    in_specs = (P("bead", None, "atom"), P(None, "bead"), P("atom"), P())
    out_specs = P("bead", None, "atom")
    return jax.shard_map(local, mesh=mesh, in_specs=in_specs, out_specs=out_specs, check_vma=False)
```

```python
import functools
import math

import jax
import jax.numpy as jnp
import numpy as np
from jax import lax
from jax.experimental import pallas as pl
from jax.experimental.pallas import tpu as pltpu
from jax.sharding import PartitionSpec as P

CONTR = 8
LANES = 128
ROWS = 16
SENT = 12
TWO_PI = 2.0 * math.pi


def polynomials():
    nodes = 0.5 * np.cos(np.pi * (np.arange(400) + 0.5) / 400)
    u = nodes * nodes
    odd = np.linalg.lstsq(
        nodes[:, None] * u[:, None] ** np.arange(7), np.sin(2 * np.pi * nodes), rcond=None
    )[0]
    even = np.linalg.lstsq(u[:, None] ** np.arange(8), np.cos(2 * np.pi * nodes), rcond=None)[0]
    return [float(c) for c in odd], [float(c) for c in even]


ODD, EVEN = polynomials()


def horner(u, coefficients):
    total = coefficients[-1]
    for c in coefficients[-2::-1]:
        total = total * u + c
    return total


def reduced(t):
    return t - jnp.round(t)


def sin_turns(t):
    t = reduced(t)
    return t * horner(t * t, ODD)


def cos_turns(t):
    t = reduced(t)
    return horner(t * t, EVEN)


def both_turns(t):
    t = reduced(t)
    u = t * t
    return horner(u, EVEN), t * horner(u, ODD)


def iota(shape, dim):
    return lax.broadcasted_iota(jnp.int32, shape, dim).astype(jnp.float32)


def pair_of(index, core):
    tile = jnp.floor(index * 0.125)
    place = index - 8.0 * tile
    run = jnp.floor((tile + 0.5) * 0.2)
    m2 = tile - 5.0 * run + 1.0 + 5.0 * core
    last = run > 2.5
    m2 = jnp.where(last, 0.0, m2)
    run = jnp.where(last, core, run)
    return m2, run_member(run, place)


def run_member(run, place):
    middle = jnp.where(place < 3, place + 8.0, -6.0 - place)
    return jnp.where(run < 0.5, place, jnp.where(run < 1.5, middle, -1.0 - place))


def place_of(m2, m3, core):
    size = jnp.abs(m3)
    outer = size > 8.5
    middle = outer | (m3 == 8.0)
    run = jnp.where(middle, 1.0, jnp.where(m3 < 0, 2.0, 0.0))
    place = jnp.where(middle, jnp.where(m3 < 0, size - 6.0, m3 - 8.0), jnp.where(m3 < 0, size - 1.0, m3))
    step = m2 - 1.0 - 5.0 * core
    row = (run * 5.0 + step) * 8.0 + place
    row = jnp.where((step >= 0) & (step < 5), row, -1.0)
    return jnp.where(m2 == 0.0, jnp.where(run == core, 120.0 + place, -1.0), row)


def split(value):
    high = value.astype(jnp.bfloat16)
    low = (value - high.astype(jnp.float32)).astype(jnp.bfloat16)
    return high, low


def dot_nt(a, b):
    return lax.dot_general(a, b, (((1,), (1,)), ((), ())), preferred_element_type=jnp.float32)


def table_value(bead, contracted, beads):
    turn = bead * (1.0 / beads) - contracted * (1.0 / CONTR)
    total = 1.0 + math.sqrt(2.0) * cos_turns(turn * (CONTR // 2))
    for mode in range(1, CONTR // 2):
        total += 2.0 * cos_turns(turn * mode)
    return total * (1.0 / beads)


def contract_kernel(
    beads_all,
    points_from,
    waves_from,
    labels_from,
    species_from,
    out_ref,
    charge_ref,
    work_ref,
    points_ref,
    waves_ref,
    labels_ref,
    species_ref,
    sems,
):
    copies_in = [
        pltpu.make_async_copy(points_from.at[x], points_ref.at[x], sems.at[x]) for x in range(3)
    ]
    for i, (source, target) in enumerate(
        ((waves_from, waves_ref), (labels_from, labels_ref), (species_from, species_ref))
    ):
        copies_in.append(pltpu.make_async_copy(source, target, sems.at[3 + i]))
    for copy in copies_in:
        copy.start()
    beads = points_ref.shape[1]
    tiles = points_ref.shape[2] // LANES
    first = (lax.axis_index("bead") * beads).astype(jnp.float32)
    columns = [
        table_value(first + b, iota((CONTR, LANES), 0), beads_all) for b in range(beads)
    ]
    for x in range(3):
        copies_in[x].wait()
        for t in range(tiles):
            block = points_ref[x, :, t * LANES : (t + 1) * LANES]
            total = columns[0] * jnp.broadcast_to(block[0:1], (CONTR, LANES))
            for b in range(1, beads):
                total += columns[b] * jnp.broadcast_to(block[b : b + 1], (CONTR, LANES))
            row = (x * tiles + t) * CONTR
            work_ref[row : row + CONTR, :] = total
    for copy in copies_in[3:]:
        copy.wait()
    waves = waves_ref[...].astype(jnp.float32)
    used = 3 * tiles
    copies = out_ref.shape[0] // CONTR
    for j in range(CONTR):
        rows = work_ref[pl.ds(j, used, stride=CONTR), :]
        for c in range(copies):
            out_ref[j * copies + c, 0:used, :] = rows
            out_ref[j * copies + c, used : used + 3, :] = waves
    labels = labels_ref[...]
    charge = jnp.zeros(labels.shape, jnp.float32)
    for kind in range(species_ref.shape[1]):
        value = jnp.broadcast_to(species_ref[:, kind : kind + 1], labels.shape)
        charge += jnp.where(labels == kind, value, 0.0)
    charge_ref[...] = charge


def own_core():
    return lax.rem(lax.axis_index("bead") + ORDERS["spots"] % 2, 2).astype(jnp.float32)


def structure_kernel(
    number_points,
    spots_ref,
    charge_ref,
    partial_ref,
    weights_ref,
    high_ref,
    low_ref,
    plain_ref,
    slope_ref,
    charged_ref,
):
    core = own_core()
    peers = spots_ref.shape[0]
    tiles = charge_ref.shape[0]
    used = 3 * tiles
    spots = spots_ref[0, 0:used, :]
    for p in range(1, peers):
        spots += spots_ref[p, 0:used, :]
    spots = reduced(spots)
    charge = charge_ref[...]
    grid_row = iota((2 * ROWS, LANES), 0)
    back = grid_row >= ROWS
    size = jnp.where(back, grid_row - ROWS, grid_row)
    wanted = jnp.where(back, jnp.where(size > 0, -size, 1000.0), size)
    pair_row = iota((LANES, LANES), 0)
    counts = jnp.zeros((2 * ROWS, LANES), jnp.float32)
    for p in range(peers):
        m1 = spots_ref[p, used : used + 1, :]
        m2 = spots_ref[p, used + 1 : used + 2, :]
        m3 = spots_ref[p, used + 2 : used + 3, :]
        sign = jnp.where(m2 < 0, -1.0, 1.0)
        fold = m2 * sign
        m3 = m3 * sign
        flip = jnp.where((fold == 0) & (m3 < 0), -1.0, 1.0)
        sign = sign * flip
        place = place_of(fold, m3 * flip, core)
        left = jnp.where(wanted == m1 * sign, 1.0, 0.0).astype(jnp.bfloat16)
        right = jnp.where(pair_row == place, 1.0, 0.0).astype(jnp.bfloat16)
        counts += dot_nt(left, right)
    m2, m3 = pair_of(iota((2 * ROWS, LANES), 1), core)
    square = size * size + m2 * m2 + m3 * m3
    square = jnp.maximum(square, 1.0)
    weights_ref[...] = counts * (4.0 * jnp.exp(square * -0.01) / (square * number_points))
    row = iota((2 * ROWS, LANES), 0)
    sine = row >= ROWS
    m1 = jnp.where(sine, row - ROWS, row)
    phase = jnp.where(sine, 0.0, 0.25)
    for t in range(tiles):
        lanes = slice(t * LANES, (t + 1) * LANES)
        x1 = spots[t : t + 1, :]
        q = charge[t : t + 1, :]
        angle = m1 * x1 + phase
        plain = q * sin_turns(angle)
        plain_ref[:, lanes] = plain
        slope_ref[:, lanes] = (q * (-TWO_PI)) * m1 * sin_turns(angle + 0.25)
        high, low = split(plain)
        charged_ref[0 : 2 * ROWS, lanes] = high
        charged_ref[2 * ROWS :, lanes] = low
    steps = 1.0 + 5.0 * core + iota((8, LANES), 0)
    runs = [run_member(jnp.full((8, LANES), float(run)), iota((8, LANES), 0)) for run in range(3)]
    for t in range(tiles):
        lanes = slice(t * LANES, (t + 1) * LANES)
        x2 = spots[tiles + t : tiles + t + 1, :]
        x3 = spots[2 * tiles + t : 2 * tiles + t + 1, :]
        cos2, sin2 = both_turns(steps * x2)
        third = [both_turns(m * x3) for m in runs]
        cosines, sines = [], []
        for run in range(3):
            cos3, sin3 = third[run]
            for i in range(5):
                c2 = jnp.broadcast_to(cos2[i : i + 1], (8, LANES))
                s2 = jnp.broadcast_to(sin2[i : i + 1], (8, LANES))
                cosines.append(c2 * cos3 - s2 * sin3)
                sines.append(s2 * cos3 + c2 * sin3)
        for values, index in ((cosines, 0), (sines, 1)):
            values.append(jnp.where(core == 0.0, third[0][index], third[1][index]))
            for r in range(0, 16, 2):
                high, low = split(jnp.concatenate(values[r : r + 2], axis=0))
                at = index * LANES + r * 8
                high_ref[at : at + 16, lanes] = high
                low_ref[at : at + 16, lanes] = low
    total = dot_nt(charged_ref[...], high_ref[...])
    total = (
        total[0 : 2 * ROWS]
        + total[2 * ROWS :]
        + dot_nt(charged_ref[0 : 2 * ROWS, :], low_ref[...])
    )
    for p in range(partial_ref.shape[0]):
        partial_ref[p, 0:SENT, :] = total[0:SENT]
        partial_ref[p, SENT:, :] = total[ROWS : ROWS + SENT]


def force_kernel(
    partial_ref, weights_ref, high_ref, low_ref, plain_ref, slope_ref, out_ref, coef_ref, term_ref
):
    core = own_core()
    tiles = plain_ref.shape[1] // LANES
    cos_row = partial_ref[0, 0:SENT, :]
    sin_row = partial_ref[0, SENT:, :]
    for p in range(1, partial_ref.shape[0]):
        cos_row += partial_ref[p, 0:SENT, :]
        sin_row += partial_ref[p, SENT:, :]
    ahead = weights_ref[0:SENT, :]
    back = weights_ref[ROWS : ROWS + SENT, :]
    cc, cs = cos_row[:, :LANES], cos_row[:, LANES:]
    sc, ss = sin_row[:, :LANES], sin_row[:, LANES:]
    ahead_cos, ahead_sin = ahead * (cc - ss), ahead * (cs + sc)
    back_cos, back_sin = back * (cc + ss), back * (cs - sc)
    m2, m3 = pair_of(iota((SENT, LANES), 1), core)
    coef_ref[...] = jnp.zeros_like(coef_ref)
    rows = (
        (ahead_cos + back_cos, ahead_sin + back_sin),
        (ahead_sin - back_sin, back_cos - ahead_cos),
    )
    for kind, (on_cos, on_sin) in enumerate(rows):
        at = kind * ROWS
        coef_ref[at : at + SENT, :LANES] = on_cos
        coef_ref[at : at + SENT, LANES:] = on_sin
        for axis, m in enumerate((m2, m3)):
            at = kind * ROWS + 2 * ROWS * (axis + 1)
            coef_ref[at : at + SENT, :LANES] = (-TWO_PI) * m * on_sin
            coef_ref[at : at + SENT, LANES:] = TWO_PI * m * on_cos
    high, low = split(coef_ref[...])
    both = jnp.concatenate([high, low], axis=0)
    size = high.shape[0]
    width = 2 * LANES
    for t in range(0, tiles, 2):
        lanes = slice(t * LANES, t * LANES + width)
        near = jnp.dot(both, high_ref[:, lanes], preferred_element_type=jnp.float32)
        far = jnp.dot(high, low_ref[:, lanes], preferred_element_type=jnp.float32)
        term = near[:size] + near[size:] + far
        plain = plain_ref[:, lanes]
        values = [term[0 : 2 * ROWS] * slope_ref[:, lanes]]
        for axis in range(2):
            at = 2 * ROWS * (axis + 1)
            values.append(term[at : at + 2 * ROWS] * plain)
        for x, value in enumerate(values):
            total = jnp.sum(value, axis=0, keepdims=True)
            for i in range(2):
                term_ref[x * tiles + t + i : x * tiles + t + i + 1, :] = total[
                    :, i * LANES : (i + 1) * LANES
                ]
    block = term_ref[...]
    for p in range(out_ref.shape[0]):
        out_ref[p, 0 : block.shape[0], :] = block


def expand_kernel(beads_all, force_ref, out_to, work_ref, out_ref, sems):
    beads = out_ref.shape[1]
    tiles = out_ref.shape[2] // LANES
    used = 3 * tiles
    stride = work_ref.shape[0] // beads
    copies = force_ref.shape[0] // CONTR
    first = (lax.axis_index("bead") * beads).astype(jnp.float32)
    rows = iota((beads * CONTR, LANES), 0)
    bead = jnp.floor((rows + 0.5) * (1.0 / CONTR))
    table = table_value(first + bead, rows - CONTR * bead, beads_all)
    done = 0
    moves = []
    for r in range(0, used, 8):
        size = min(8, used - r)
        parts = []
        for j in range(CONTR):
            turn = ORDERS["spots"] ^ ORDERS["forces"]
            part = force_ref[(j * copies) ^ turn, r : r + size, :]
            for c in range(1, copies):
                part += force_ref[(j * copies + c) ^ turn, r : r + size, :]
            parts.append(part)
        for b in range(beads):
            at = b * CONTR
            total = parts[0] * table[at : at + 1]
            for j in range(1, CONTR):
                total += parts[j] * table[at + j : at + j + 1]
            work_ref[b * stride + r : b * stride + r + size, :] = total
        for i in range(r, r + size):
            x, t = divmod(i, tiles)
            out_ref[x, :, t * LANES : (t + 1) * LANES] = work_ref[
                pl.ds(i, beads, stride=stride), :
            ]
        while done < 3 and (done + 1) * tiles <= r + size:
            moves.append(pltpu.make_async_copy(out_ref.at[done], out_to.at[done], sems.at[done]))
            moves[-1].start()
            done += 1
    for move in moves:
        move.wait()


VMEM = pl.BlockSpec(memory_space=pltpu.VMEM)
HBM = pl.BlockSpec(memory_space=pltpu.HBM)
PARAMS = pltpu.CompilerParams(vmem_limit_bytes=24 * 1024 * 1024)


ORDERS = {"spots": 14, "factors": 5, "forces": 15}


def exchange(array, axis, key):
    order = [i ^ ORDERS[key] for i in range(lax.axis_size(axis))]
    return lax.all_to_all(array, axis, 0, 0, axis_index_groups=[order], tiled=True)


def shaped(*shape, dtype=jnp.float32):
    return jax.ShapeDtypeStruct(shape, dtype)


def local(points, waves, labels, species):
    beads, _, sites = points.shape
    bead_peers = lax.axis_size("bead")
    atom_peers = lax.axis_size("atom")
    tiles = sites // LANES
    used = 3 * tiles
    sent = -(-(used + 3) // 8) * 8
    held = -(-used // 8) * 8
    beads_all = beads * bead_peers
    portion, charge = pl.pallas_call(
        functools.partial(contract_kernel, beads_all),
        out_shape=[shaped(bead_peers, sent, LANES), shaped(tiles, LANES)],
        in_specs=[HBM] * 4,
        out_specs=[VMEM] * 2,
        scratch_shapes=[
            pltpu.VMEM((used * CONTR, LANES), jnp.float32),
            pltpu.VMEM((3, beads, sites), jnp.float32),
            pltpu.VMEM(waves.shape, jnp.int32),
            pltpu.VMEM((tiles, LANES), jnp.int32),
            pltpu.VMEM((1, species.shape[0]), jnp.float32),
            pltpu.SemaphoreType.DMA((6,)),
        ],
        compiler_params=PARAMS,
        name="contract",
    )(
        *(
            pltpu.with_memory_space_constraint(a, pltpu.HBM)
            for a in (
                points.transpose(1, 0, 2),
                waves,
                labels.reshape(tiles, LANES),
                species[None, :],
            )
        )
    )
    spots = exchange(portion, "bead", "spots")
    partial, weights, high, low, plain, slope = pl.pallas_call(
        functools.partial(structure_kernel, float(sites * atom_peers)),
        out_shape=[
            shaped(atom_peers, 2 * SENT, 2 * LANES),
            shaped(2 * ROWS, LANES),
            shaped(2 * LANES, sites, dtype=jnp.bfloat16),
            shaped(2 * LANES, sites, dtype=jnp.bfloat16),
            shaped(2 * ROWS, sites),
            shaped(2 * ROWS, sites),
        ],
        in_specs=[VMEM] * 2,
        out_specs=[VMEM] * 6,
        scratch_shapes=[pltpu.VMEM((4 * ROWS, sites), jnp.bfloat16)],
        compiler_params=PARAMS,
        name="structure",
    )(spots, charge)
    factors = exchange(partial, "atom", "factors")
    force = pl.pallas_call(
        force_kernel,
        out_shape=shaped(bead_peers, held, LANES),
        in_specs=[VMEM] * 6,
        out_specs=VMEM,
        scratch_shapes=[
            pltpu.VMEM((6 * ROWS, 2 * LANES), jnp.float32),
            pltpu.VMEM((used, LANES), jnp.float32),
        ],
        compiler_params=PARAMS,
        name="force",
    )(factors, weights, high, low, plain, slope)
    forces = exchange(force, "bead", "forces")
    out = pl.pallas_call(
        functools.partial(expand_kernel, beads_all),
        out_shape=shaped(3, beads, sites),
        in_specs=[VMEM],
        out_specs=HBM,
        scratch_shapes=[
            pltpu.VMEM((beads * held, LANES), jnp.float32),
            pltpu.VMEM((3, beads, sites), jnp.float32),
            pltpu.SemaphoreType.DMA((3,)),
        ],
        compiler_params=PARAMS,
        name="expand",
    )(forces)
    return out.transpose(1, 0, 2)


def solution(mesh):
    in_specs = (P("bead", None, "atom"), P(None, "bead"), P("atom"), P())
    out_specs = P("bead", None, "atom")
    return jax.shard_map(local, mesh=mesh, in_specs=in_specs, out_specs=out_specs, check_vma=False)
```

```python
import functools
import math

import jax
import jax.numpy as jnp
import numpy as np
from jax import lax
from jax.experimental import pallas as pl
from jax.experimental.pallas import tpu as pltpu
from jax.sharding import PartitionSpec as P

CONTR = 8
LANES = 128
ROWS = 16
SENT = 12
TWO_PI = 2.0 * math.pi


def polynomials():
    nodes = 0.5 * np.cos(np.pi * (np.arange(400) + 0.5) / 400)
    u = nodes * nodes
    odd = np.linalg.lstsq(
        nodes[:, None] * u[:, None] ** np.arange(7), np.sin(2 * np.pi * nodes), rcond=None
    )[0]
    even = np.linalg.lstsq(u[:, None] ** np.arange(8), np.cos(2 * np.pi * nodes), rcond=None)[0]
    return [float(c) for c in odd], [float(c) for c in even]


ODD, EVEN = polynomials()


def horner(u, coefficients):
    total = coefficients[-1]
    for c in coefficients[-2::-1]:
        total = total * u + c
    return total


def reduced(t):
    return t - jnp.round(t)


def sin_turns(t):
    t = reduced(t)
    return t * horner(t * t, ODD)


def cos_turns(t):
    t = reduced(t)
    return horner(t * t, EVEN)


def both_turns(t):
    t = reduced(t)
    u = t * t
    return horner(u, EVEN), t * horner(u, ODD)


def iota(shape, dim):
    return lax.broadcasted_iota(jnp.int32, shape, dim).astype(jnp.float32)


def pair_of(index, core):
    tile = jnp.floor(index * 0.125)
    place = index - 8.0 * tile
    run = jnp.floor((tile + 0.5) * 0.2)
    m2 = tile - 5.0 * run + 1.0 + 5.0 * core
    last = run > 2.5
    m2 = jnp.where(last, 0.0, m2)
    run = jnp.where(last, core, run)
    return m2, run_member(run, place)


def run_member(run, place):
    middle = jnp.where(place < 0.5, 0.0, jnp.where(place < 2.5, place + 8.0, -6.0 - place))
    return jnp.where(run < 0.5, place + 1.0, jnp.where(run < 1.5, middle, -1.0 - place))


def place_of(m2, m3, core):
    size = jnp.abs(m3)
    middle = (size > 8.5) | (size < 0.5)
    run = jnp.where(middle, 1.0, jnp.where(m3 < 0, 2.0, 0.0))
    inner = jnp.where(m3 < 0, size - 6.0, jnp.maximum(size - 8.0, 0.0))
    place = jnp.where(middle, inner, size - 1.0)
    step = m2 - 1.0 - 5.0 * core
    row = (run * 5.0 + step) * 8.0 + place
    row = jnp.where((step >= 0) & (step < 5), row, -1.0)
    return jnp.where(m2 == 0.0, jnp.where(run == core, 120.0 + place, -1.0), row)


def split(value):
    high = value.astype(jnp.bfloat16)
    low = (value - high.astype(jnp.float32)).astype(jnp.bfloat16)
    return high, low


def dot_nt(a, b):
    return lax.dot_general(a, b, (((1,), (1,)), ((), ())), preferred_element_type=jnp.float32)


def table_value(bead, contracted, beads):
    turn = bead * (1.0 / beads) - contracted * (1.0 / CONTR)
    total = 1.0 + math.sqrt(2.0) * cos_turns(turn * (CONTR // 2))
    for mode in range(1, CONTR // 2):
        total += 2.0 * cos_turns(turn * mode)
    return total * (1.0 / beads)


def contract_kernel(
    beads_all,
    points_from,
    waves_from,
    labels_from,
    species_from,
    out_ref,
    charge_ref,
    table_ref,
    work_ref,
    points_ref,
    waves_ref,
    labels_ref,
    species_ref,
    sems,
):
    copies_in = [
        pltpu.make_async_copy(points_from.at[x], points_ref.at[x], sems.at[x]) for x in range(3)
    ]
    for i, (source, target) in enumerate(
        ((waves_from, waves_ref), (labels_from, labels_ref), (species_from, species_ref))
    ):
        copies_in.append(pltpu.make_async_copy(source, target, sems.at[3 + i]))
    for copy in copies_in:
        copy.start()
    beads = points_ref.shape[1]
    tiles = points_ref.shape[2] // LANES
    first = (lax.axis_index("bead") * beads).astype(jnp.float32)
    columns = [
        table_value(first + b, iota((CONTR, LANES), 0), beads_all) for b in range(beads)
    ]
    for b in range(beads):
        table_ref[b * CONTR : (b + 1) * CONTR, :] = columns[b]
    for x in range(3):
        copies_in[x].wait()
        for t in range(tiles):
            block = points_ref[x, :, t * LANES : (t + 1) * LANES]
            total = columns[0] * jnp.broadcast_to(block[0:1], (CONTR, LANES))
            for b in range(1, beads):
                total += columns[b] * jnp.broadcast_to(block[b : b + 1], (CONTR, LANES))
            row = (x * tiles + t) * CONTR
            work_ref[row : row + CONTR, :] = total
    for copy in copies_in[3:]:
        copy.wait()
    waves = waves_ref[...].astype(jnp.float32)
    used = 3 * tiles
    copies = out_ref.shape[0] // CONTR
    for j in range(CONTR):
        rows = work_ref[pl.ds(j, used, stride=CONTR), :]
        for c in range(copies):
            out_ref[j * copies + c, 0:used, :] = rows
            out_ref[j * copies + c, used : used + 3, :] = waves
    labels = labels_ref[...]
    charge = jnp.zeros(labels.shape, jnp.float32)
    for kind in range(species_ref.shape[1]):
        value = jnp.broadcast_to(species_ref[:, kind : kind + 1], labels.shape)
        charge += jnp.where(labels == kind, value, 0.0)
    charge_ref[...] = charge


def own_core():
    bits, first = ORDERS["spots"]
    scale = 1 << bits[0]
    bit = lax.rem(lax.div(lax.axis_index("bead"), scale), 2)
    return (1 - bit if first & scale else bit).astype(jnp.float32)


def structure_kernel(
    number_points,
    spots_ref,
    charge_ref,
    partial_ref,
    weights_ref,
    high_ref,
    low_ref,
    plain_ref,
    charged_ref,
):
    core = own_core()
    peers = spots_ref.shape[0]
    tiles = charge_ref.shape[0]
    used = 3 * tiles
    spots = spots_ref[0, 0:used, :]
    for p in range(1, peers):
        spots += spots_ref[p, 0:used, :]
    spots = reduced(spots)
    charge = charge_ref[...]
    grid_row = iota((2 * ROWS, LANES), 0)
    back = grid_row >= ROWS
    size = jnp.where(back, grid_row - ROWS, grid_row)
    wanted = jnp.where(back, jnp.where(size > 0, -size, 1000.0), size)
    pair_row = iota((LANES, LANES), 0)
    m1, m2, m3 = (spots_ref[:, used + x, :] for x in range(3))
    sign = jnp.where(m2 < 0, -1.0, 1.0)
    sign = jnp.where((m2 == 0) & (m3 < 0), -1.0, sign)
    m1 = m1 * sign
    place = place_of(m2 * sign, m3 * sign, core)
    counts = jnp.zeros((2 * ROWS, LANES), jnp.float32)
    for p in range(peers):
        left = jnp.where(wanted == m1[p : p + 1], 1.0, 0.0).astype(jnp.bfloat16)
        right = jnp.where(pair_row == place[p : p + 1], 1.0, 0.0).astype(jnp.bfloat16)
        counts += dot_nt(left, right)
    m2, m3 = pair_of(iota((2 * ROWS, LANES), 1), core)
    square = size * size + m2 * m2 + m3 * m3
    square = jnp.maximum(square, 1.0)
    weights_ref[...] = counts * (4.0 * jnp.exp(square * -0.01) / (square * number_points))
    size = iota((ROWS, LANES), 0)
    steps = 1.0 + 5.0 * core + iota((8, LANES), 0)
    place = iota((8, LANES), 0)
    outer, middle = (run_member(jnp.full((8, LANES), run), place) for run in (0.0, 1.0))
    for t in range(tiles):
        lanes = slice(t * LANES, (t + 1) * LANES)
        x1 = spots[t : t + 1, :]
        x2 = spots[tiles + t : tiles + t + 1, :]
        x3 = spots[2 * tiles + t : 2 * tiles + t + 1, :]
        q = charge[t : t + 1, :]
        for index, value in enumerate(both_turns(size * x1)):
            value = q * value
            at = index * ROWS
            plain_ref[at : at + ROWS, lanes] = value
            high, low = split(value)
            charged_ref[at : at + ROWS, lanes] = high
            charged_ref[2 * ROWS + at : 3 * ROWS + at, lanes] = low
        cos2, sin2 = both_turns(steps * x2)
        cos3, sin3 = both_turns(outer * x3)
        cos4, sin4 = both_turns(middle * x3)
        cosines, sines = [None] * 15, [None] * 15
        for i in range(5):
            c2 = jnp.broadcast_to(cos2[i : i + 1], (8, LANES))
            s2 = jnp.broadcast_to(sin2[i : i + 1], (8, LANES))
            cc, ss, sc, cs = c2 * cos3, s2 * sin3, s2 * cos3, c2 * sin3
            cosines[i], sines[i] = cc - ss, sc + cs
            cosines[5 + i], sines[5 + i] = c2 * cos4 - s2 * sin4, s2 * cos4 + c2 * sin4
            cosines[10 + i], sines[10 + i] = cc + ss, sc - cs
        cosines.append(jnp.where(core == 0.0, cos3, cos4))
        sines.append(jnp.where(core == 0.0, sin3, sin4))
        for index, values in enumerate((cosines, sines)):
            for r in range(0, 16, 2):
                high, low = split(jnp.concatenate(values[r : r + 2], axis=0))
                at = index * LANES + r * 8
                high_ref[at : at + 16, lanes] = high
                low_ref[at : at + 16, lanes] = low
    total = dot_nt(charged_ref[...], high_ref[...])
    total = (
        total[0 : 2 * ROWS]
        + total[2 * ROWS :]
        + dot_nt(charged_ref[0 : 2 * ROWS, :], low_ref[...])
    )
    for p in range(partial_ref.shape[0]):
        partial_ref[p, 0:SENT, :] = total[0:SENT]
        partial_ref[p, SENT:, :] = total[ROWS : ROWS + SENT]


def force_kernel(
    partial_ref, weights_ref, high_ref, low_ref, plain_ref, out_ref, coef_ref, term_ref
):
    core = own_core()
    tiles = plain_ref.shape[1] // LANES
    cos_row = partial_ref[0, 0:SENT, :]
    sin_row = partial_ref[0, SENT:, :]
    for p in range(1, partial_ref.shape[0]):
        cos_row += partial_ref[p, 0:SENT, :]
        sin_row += partial_ref[p, SENT:, :]
    ahead = weights_ref[0:SENT, :]
    back = weights_ref[ROWS : ROWS + SENT, :]
    cc, cs = cos_row[:, :LANES], cos_row[:, LANES:]
    sc, ss = sin_row[:, :LANES], sin_row[:, LANES:]
    ahead_cos, ahead_sin = ahead * (cc - ss), ahead * (cs + sc)
    back_cos, back_sin = back * (cc + ss), back * (cs - sc)
    m2, m3 = pair_of(iota((SENT, LANES), 1), core)
    coef_ref[...] = jnp.zeros_like(coef_ref)
    rows = (
        (ahead_cos + back_cos, ahead_sin + back_sin),
        (ahead_sin - back_sin, back_cos - ahead_cos),
    )
    m1 = TWO_PI * iota((SENT, LANES), 0)
    for kind, (on_cos, on_sin) in enumerate(rows):
        at = (1 - kind) * ROWS
        along = m1 if kind == 0 else -m1
        coef_ref[at : at + SENT, :LANES] = along * on_cos
        coef_ref[at : at + SENT, LANES:] = along * on_sin
        for axis, m in enumerate((m2, m3)):
            at = kind * ROWS + 2 * ROWS * (axis + 1)
            coef_ref[at : at + SENT, :LANES] = (-TWO_PI) * m * on_sin
            coef_ref[at : at + SENT, LANES:] = TWO_PI * m * on_cos
    high, low = split(coef_ref[...])
    both = jnp.concatenate([high, low], axis=0)
    size = high.shape[0]
    width = 2 * LANES
    for t in range(0, tiles, 2):
        lanes = slice(t * LANES, t * LANES + width)
        near = jnp.dot(both, high_ref[:, lanes], preferred_element_type=jnp.float32)
        far = jnp.dot(high, low_ref[:, lanes], preferred_element_type=jnp.float32)
        term = near[:size] + near[size:] + far
        plain = plain_ref[:, lanes]
        for x in range(3):
            at = 2 * ROWS * x
            total = jnp.sum(term[at : at + 2 * ROWS] * plain, axis=0, keepdims=True)
            for i in range(2):
                term_ref[x * tiles + t + i : x * tiles + t + i + 1, :] = total[
                    :, i * LANES : (i + 1) * LANES
                ]
    block = term_ref[...]
    for p in range(out_ref.shape[0]):
        out_ref[p, 0 : block.shape[0], :] = block


def expand_kernel(table_ref, force_ref, out_to, work_ref, out_ref, sems):
    beads = out_ref.shape[1]
    tiles = out_ref.shape[2] // LANES
    used = 3 * tiles
    stride = work_ref.shape[0] // beads
    copies = force_ref.shape[0] // CONTR
    table = table_ref[...]
    arrivals = members("forces")
    senders = [arrivals.index(member) for member in members("spots")]
    done = 0
    moves = []
    for r in range(0, used, 8):
        size = min(8, used - r)
        parts = []
        for j in range(CONTR):
            part = force_ref[senders[j * copies], r : r + size, :]
            for c in range(1, copies):
                part += force_ref[senders[j * copies + c], r : r + size, :]
            parts.append(part)
        for b in range(beads):
            at = b * CONTR
            total = parts[0] * table[at : at + 1]
            for j in range(1, CONTR):
                total += parts[j] * table[at + j : at + j + 1]
            work_ref[b * stride + r : b * stride + r + size, :] = total
        for i in range(r, r + size):
            x, t = divmod(i, tiles)
            out_ref[x, :, t * LANES : (t + 1) * LANES] = work_ref[
                pl.ds(i, beads, stride=stride), :
            ]
        while done < 3 and (done + 1) * tiles <= r + size:
            moves.append(pltpu.make_async_copy(out_ref.at[done], out_to.at[done], sems.at[done]))
            moves[-1].start()
            done += 1
    for move in moves:
        move.wait()


VMEM = pl.BlockSpec(memory_space=pltpu.VMEM)
HBM = pl.BlockSpec(memory_space=pltpu.HBM)
PARAMS = pltpu.CompilerParams(vmem_limit_bytes=24 * 1024 * 1024)


ORDERS = {
    "spots": ((0, 1, 2, 3), 14),
    "factors": ((0, 1, 2), 5),
    "forces": ((0, 1, 2, 3), 15),
}


def members(key):
    bits, first = ORDERS[key]
    return [
        sum((place >> i & 1) << bit for i, bit in enumerate(bits)) ^ first
        for place in range(1 << len(bits))
    ]


def exchange(array, axis, key):
    return lax.all_to_all(
        array, axis, 0, 0, axis_index_groups=[members(key)], tiled=True
    )


def shaped(*shape, dtype=jnp.float32):
    return jax.ShapeDtypeStruct(shape, dtype)


def local(points, waves, labels, species):
    beads, _, sites = points.shape
    bead_peers = lax.axis_size("bead")
    atom_peers = lax.axis_size("atom")
    tiles = sites // LANES
    used = 3 * tiles
    sent = -(-(used + 3) // 8) * 8
    held = -(-used // 8) * 8
    beads_all = beads * bead_peers
    portion, charge, table = pl.pallas_call(
        functools.partial(contract_kernel, beads_all),
        out_shape=[
            shaped(bead_peers, sent, LANES),
            shaped(tiles, LANES),
            shaped(beads * CONTR, LANES),
        ],
        in_specs=[HBM] * 4,
        out_specs=[VMEM] * 3,
        scratch_shapes=[
            pltpu.VMEM((used * CONTR, LANES), jnp.float32),
            pltpu.VMEM((3, beads, sites), jnp.float32),
            pltpu.VMEM(waves.shape, jnp.int32),
            pltpu.VMEM((tiles, LANES), jnp.int32),
            pltpu.VMEM((1, species.shape[0]), jnp.float32),
            pltpu.SemaphoreType.DMA((6,)),
        ],
        compiler_params=PARAMS,
        name="contract",
    )(
        *(
            pltpu.with_memory_space_constraint(a, pltpu.HBM)
            for a in (
                points.transpose(1, 0, 2),
                waves,
                labels.reshape(tiles, LANES),
                species[None, :],
            )
        )
    )
    spots = exchange(portion, "bead", "spots")
    partial, weights, high, low, plain = pl.pallas_call(
        functools.partial(structure_kernel, float(sites * atom_peers)),
        out_shape=[
            shaped(atom_peers, 2 * SENT, 2 * LANES),
            shaped(2 * ROWS, LANES),
            shaped(2 * LANES, sites, dtype=jnp.bfloat16),
            shaped(2 * LANES, sites, dtype=jnp.bfloat16),
            shaped(2 * ROWS, sites),
        ],
        in_specs=[VMEM] * 2,
        out_specs=[VMEM] * 5,
        scratch_shapes=[pltpu.VMEM((4 * ROWS, sites), jnp.bfloat16)],
        compiler_params=PARAMS,
        name="structure",
    )(spots, charge)
    factors = exchange(partial, "atom", "factors")
    force = pl.pallas_call(
        force_kernel,
        out_shape=shaped(bead_peers, held, LANES),
        in_specs=[VMEM] * 5,
        out_specs=VMEM,
        scratch_shapes=[
            pltpu.VMEM((6 * ROWS, 2 * LANES), jnp.float32),
            pltpu.VMEM((used, LANES), jnp.float32),
        ],
        compiler_params=PARAMS,
        name="force",
    )(factors, weights, high, low, plain)
    forces = exchange(force, "bead", "forces")
    out = pl.pallas_call(
        expand_kernel,
        out_shape=shaped(3, beads, sites),
        in_specs=[VMEM] * 2,
        out_specs=HBM,
        scratch_shapes=[
            pltpu.VMEM((beads * held, LANES), jnp.float32),
            pltpu.VMEM((3, beads, sites), jnp.float32),
            pltpu.SemaphoreType.DMA((3,)),
        ],
        compiler_params=PARAMS,
        name="expand",
    )(table, forces)
    return out.transpose(1, 0, 2)


def solution(mesh):
    in_specs = (P("bead", None, "atom"), P(None, "bead"), P("atom"), P())
    out_specs = P("bead", None, "atom")
    return jax.shard_map(local, mesh=mesh, in_specs=in_specs, out_specs=out_specs, check_vma=False)
```

```python
import functools
import math

import jax
import jax.numpy as jnp
import numpy as np
from jax import lax
from jax.experimental import pallas as pl
from jax.experimental.pallas import tpu as pltpu
from jax.sharding import PartitionSpec as P

CONTR = 8
LANES = 128
ROWS = 16
SENT = 12
TWO_PI = 2.0 * math.pi


def polynomials():
    nodes = 0.5 * np.cos(np.pi * (np.arange(400) + 0.5) / 400)
    u = nodes * nodes
    odd = np.linalg.lstsq(
        nodes[:, None] * u[:, None] ** np.arange(7), np.sin(2 * np.pi * nodes), rcond=None
    )[0]
    even = np.linalg.lstsq(u[:, None] ** np.arange(8), np.cos(2 * np.pi * nodes), rcond=None)[0]
    return [float(c) for c in odd], [float(c) for c in even]


ODD, EVEN = polynomials()


def horner(u, coefficients):
    total = coefficients[-1]
    for c in coefficients[-2::-1]:
        total = total * u + c
    return total


def reduced(t):
    return t - jnp.round(t)


def sin_turns(t):
    t = reduced(t)
    return t * horner(t * t, ODD)


def cos_turns(t):
    t = reduced(t)
    return horner(t * t, EVEN)


def both_turns(t):
    t = reduced(t)
    u = t * t
    return horner(u, EVEN), t * horner(u, ODD)


def iota(shape, dim):
    return lax.broadcasted_iota(jnp.int32, shape, dim).astype(jnp.float32)


def pair_of(index, core):
    tile = jnp.floor(index * 0.125)
    place = index - 8.0 * tile
    run = jnp.floor((tile + 0.5) * 0.2)
    m2 = tile - 5.0 * run + 1.0 + 5.0 * core
    last = run > 2.5
    m2 = jnp.where(last, 0.0, m2)
    run = jnp.where(last, core, run)
    return m2, run_member(run, place)


def run_member(run, place):
    middle = jnp.where(place < 0.5, 0.0, jnp.where(place < 2.5, place + 8.0, -6.0 - place))
    return jnp.where(run < 0.5, place + 1.0, jnp.where(run < 1.5, middle, -1.0 - place))


def place_of(m2, m3, core):
    size = jnp.abs(m3)
    middle = (size > 8.5) | (size < 0.5)
    run = jnp.where(middle, 1.0, jnp.where(m3 < 0, 2.0, 0.0))
    inner = jnp.where(m3 < 0, size - 6.0, jnp.maximum(size - 8.0, 0.0))
    place = jnp.where(middle, inner, size - 1.0)
    step = m2 - 1.0 - 5.0 * core
    row = (run * 5.0 + step) * 8.0 + place
    row = jnp.where((step >= 0) & (step < 5), row, -1.0)
    return jnp.where(m2 == 0.0, jnp.where(run == core, 120.0 + place, -1.0), row)


def split(value):
    high = value.astype(jnp.bfloat16)
    low = (value - high.astype(jnp.float32)).astype(jnp.bfloat16)
    return high, low


def dot_nt(a, b):
    return lax.dot_general(a, b, (((1,), (1,)), ((), ())), preferred_element_type=jnp.float32)


def table_value(bead, contracted, beads):
    turn = bead * (1.0 / beads) - contracted * (1.0 / CONTR)
    total = 1.0 + math.sqrt(2.0) * cos_turns(turn * (CONTR // 2))
    for mode in range(1, CONTR // 2):
        total += 2.0 * cos_turns(turn * mode)
    return total * (1.0 / beads)


def contract_kernel(
    beads_all,
    points_from,
    waves_from,
    labels_from,
    species_from,
    kept_ref,
    given_ref,
    charge_ref,
    table_ref,
    work_ref,
    points_ref,
    waves_ref,
    labels_ref,
    species_ref,
    sems,
):
    copies_in = [
        pltpu.make_async_copy(points_from.at[x], points_ref.at[x], sems.at[x]) for x in range(3)
    ]
    for i, (source, target) in enumerate(
        ((waves_from, waves_ref), (labels_from, labels_ref), (species_from, species_ref))
    ):
        copies_in.append(pltpu.make_async_copy(source, target, sems.at[3 + i]))
    for copy in copies_in:
        copy.start()
    beads = points_ref.shape[1]
    tiles = points_ref.shape[2] // LANES
    bead_index = lax.axis_index("bead")
    first = (bead_index * beads).astype(jnp.float32)
    start = (lax.rem(bead_index, 2) * (CONTR // 2)).astype(jnp.float32)
    columns = [
        table_value(first + b, iota((CONTR, LANES), 0) + start, beads_all) for b in range(beads)
    ]
    for b in range(beads):
        table_ref[b * CONTR : (b + 1) * CONTR, :] = columns[b]
    for x in range(3):
        copies_in[x].wait()
        for t in range(tiles):
            block = points_ref[x, :, t * LANES : (t + 1) * LANES]
            total = columns[0] * jnp.broadcast_to(block[0:1], (CONTR, LANES))
            for b in range(1, beads):
                total += columns[b] * jnp.broadcast_to(block[b : b + 1], (CONTR, LANES))
            row = (x * tiles + t) * CONTR
            work_ref[row : row + CONTR, :] = total
    used = 3 * tiles
    half = CONTR // 2
    for target, begin in ((given_ref, half), (kept_ref, 0)):
        for j in range(half):
            target[j, 0:used, :] = work_ref[pl.ds(begin + j, used, stride=CONTR), :]
    for copy in copies_in[3:]:
        copy.wait()
    waves = waves_ref[...].astype(jnp.float32)
    for target in (given_ref, kept_ref):
        target[0, used : used + 3, :] = waves
    labels = labels_ref[...]
    charge = jnp.zeros(labels.shape, jnp.float32)
    for kind in range(species_ref.shape[1]):
        value = jnp.broadcast_to(species_ref[:, kind : kind + 1], labels.shape)
        charge += jnp.where(labels == kind, value, 0.0)
    charge_ref[...] = charge


def pair_sum_kernel(used, kept_ref, taken_ref, out_ref):
    copies = out_ref.shape[0] // kept_ref.shape[0]
    kept_waves = kept_ref[0, used : used + 3, :]
    taken_waves = taken_ref[0, used : used + 3, :]
    for j in range(kept_ref.shape[0]):
        total = kept_ref[j, 0:used, :] + taken_ref[j, 0:used, :]
        for c in range(copies):
            out_ref[j * copies + c, 0:used, :] = total
            out_ref[j * copies + c, used : used + 3, :] = kept_waves
            out_ref[j * copies + c, used + 3 : used + 6, :] = taken_waves


def own_half():
    first = ORDERS["spots"]
    bit = lax.rem(lax.div(lax.axis_index("bead"), 2) + first % 2, 2)
    return bit.astype(jnp.float32)


def structure_kernel(
    number_points,
    spots_ref,
    charge_ref,
    partial_ref,
    weights_ref,
    high_ref,
    low_ref,
    plain_ref,
    charged_ref,
):
    half = own_half()
    peers = spots_ref.shape[0]
    tiles = charge_ref.shape[0]
    used = 3 * tiles
    spots = spots_ref[0, 0:used, :]
    for p in range(1, peers):
        spots += spots_ref[p, 0:used, :]
    spots = reduced(spots)
    charge = charge_ref[...]
    grid_row = iota((2 * ROWS, LANES), 0)
    back = grid_row >= ROWS
    size = jnp.where(back, grid_row - ROWS, grid_row)
    wanted = jnp.where(back, jnp.where(size > 0, -size, 1000.0), size)
    pair_row = iota((LANES, LANES), 0)
    m1, m2, m3 = (
        jnp.concatenate([spots_ref[:, used + x, :], spots_ref[:, used + 3 + x, :]], axis=0)
        for x in range(3)
    )
    sign = jnp.where(m2 < 0, -1.0, 1.0)
    sign = jnp.where((m2 == 0) & (m3 < 0), -1.0, sign)
    m1 = m1 * sign
    place = place_of(m2 * sign, m3 * sign, half)
    counts = jnp.zeros((2 * ROWS, LANES), jnp.float32)
    for p in range(2 * peers):
        left = jnp.where(wanted == m1[p : p + 1], 1.0, 0.0).astype(jnp.bfloat16)
        right = jnp.where(pair_row == place[p : p + 1], 1.0, 0.0).astype(jnp.bfloat16)
        counts += dot_nt(left, right)
    m2, m3 = pair_of(iota((2 * ROWS, LANES), 1), half)
    square = size * size + m2 * m2 + m3 * m3
    square = jnp.maximum(square, 1.0)
    weights_ref[...] = counts * (4.0 * jnp.exp(square * -0.01) / (square * number_points))
    size = iota((ROWS, LANES), 0)
    steps = 1.0 + 5.0 * half + iota((8, LANES), 0)
    place = iota((8, LANES), 0)
    outer, middle = (run_member(jnp.full((8, LANES), run), place) for run in (0.0, 1.0))
    for t in range(tiles):
        lanes = slice(t * LANES, (t + 1) * LANES)
        x1 = spots[t : t + 1, :]
        x2 = spots[tiles + t : tiles + t + 1, :]
        x3 = spots[2 * tiles + t : 2 * tiles + t + 1, :]
        q = charge[t : t + 1, :]
        for index, value in enumerate(both_turns(size * x1)):
            value = q * value
            at = index * ROWS
            plain_ref[at : at + ROWS, lanes] = value
            high, low = split(value)
            charged_ref[at : at + ROWS, lanes] = high
            charged_ref[2 * ROWS + at : 3 * ROWS + at, lanes] = low
        cos2, sin2 = both_turns(steps * x2)
        cos3, sin3 = both_turns(outer * x3)
        cos4, sin4 = both_turns(middle * x3)
        cosines, sines = [None] * 15, [None] * 15
        for i in range(5):
            c2 = jnp.broadcast_to(cos2[i : i + 1], (8, LANES))
            s2 = jnp.broadcast_to(sin2[i : i + 1], (8, LANES))
            cc, ss, sc, cs = c2 * cos3, s2 * sin3, s2 * cos3, c2 * sin3
            cosines[i], sines[i] = cc - ss, sc + cs
            cosines[5 + i], sines[5 + i] = c2 * cos4 - s2 * sin4, s2 * cos4 + c2 * sin4
            cosines[10 + i], sines[10 + i] = cc + ss, sc - cs
        cosines.append(jnp.where(half == 0.0, cos3, cos4))
        sines.append(jnp.where(half == 0.0, sin3, sin4))
        for index, values in enumerate((cosines, sines)):
            for r in range(0, 16, 2):
                high, low = split(jnp.concatenate(values[r : r + 2], axis=0))
                at = index * LANES + r * 8
                high_ref[at : at + 16, lanes] = high
                low_ref[at : at + 16, lanes] = low
    total = dot_nt(charged_ref[...], high_ref[...])
    total = (
        total[0 : 2 * ROWS]
        + total[2 * ROWS :]
        + dot_nt(charged_ref[0 : 2 * ROWS, :], low_ref[...])
    )
    for p in range(partial_ref.shape[0]):
        partial_ref[p, 0:SENT, :] = total[0:SENT]
        partial_ref[p, SENT:, :] = total[ROWS : ROWS + SENT]


def force_kernel(
    partial_ref, weights_ref, high_ref, low_ref, plain_ref, out_ref, coef_ref, term_ref
):
    half = own_half()
    tiles = plain_ref.shape[1] // LANES
    cos_row = partial_ref[0, 0:SENT, :]
    sin_row = partial_ref[0, SENT:, :]
    for p in range(1, partial_ref.shape[0]):
        cos_row += partial_ref[p, 0:SENT, :]
        sin_row += partial_ref[p, SENT:, :]
    ahead = weights_ref[0:SENT, :]
    back = weights_ref[ROWS : ROWS + SENT, :]
    cc, cs = cos_row[:, :LANES], cos_row[:, LANES:]
    sc, ss = sin_row[:, :LANES], sin_row[:, LANES:]
    ahead_cos, ahead_sin = ahead * (cc - ss), ahead * (cs + sc)
    back_cos, back_sin = back * (cc + ss), back * (cs - sc)
    m2, m3 = pair_of(iota((SENT, LANES), 1), half)
    coef_ref[...] = jnp.zeros_like(coef_ref)
    rows = (
        (ahead_cos + back_cos, ahead_sin + back_sin),
        (ahead_sin - back_sin, back_cos - ahead_cos),
    )
    m1 = TWO_PI * iota((SENT, LANES), 0)
    for kind, (on_cos, on_sin) in enumerate(rows):
        at = (1 - kind) * ROWS
        along = m1 if kind == 0 else -m1
        coef_ref[at : at + SENT, :LANES] = along * on_cos
        coef_ref[at : at + SENT, LANES:] = along * on_sin
        for axis, m in enumerate((m2, m3)):
            at = kind * ROWS + 2 * ROWS * (axis + 1)
            coef_ref[at : at + SENT, :LANES] = (-TWO_PI) * m * on_sin
            coef_ref[at : at + SENT, LANES:] = TWO_PI * m * on_cos
    high, low = split(coef_ref[...])
    both = jnp.concatenate([high, low], axis=0)
    size = high.shape[0]
    width = 2 * LANES
    for t in range(0, tiles, 2):
        lanes = slice(t * LANES, t * LANES + width)
        near = jnp.dot(both, high_ref[:, lanes], preferred_element_type=jnp.float32)
        far = jnp.dot(high, low_ref[:, lanes], preferred_element_type=jnp.float32)
        term = near[:size] + near[size:] + far
        plain = plain_ref[:, lanes]
        for x in range(3):
            at = 2 * ROWS * x
            total = jnp.sum(term[at : at + 2 * ROWS] * plain, axis=0, keepdims=True)
            for i in range(2):
                term_ref[x * tiles + t + i : x * tiles + t + i + 1, :] = total[
                    :, i * LANES : (i + 1) * LANES
                ]
    block = term_ref[...]
    for p in range(out_ref.shape[0]):
        out_ref[p, 0 : block.shape[0], :] = block


def gather_kernel(used, force_ref, out_ref):
    arrivals = members("forces")
    senders = [arrivals.index(member) for member in members("spots")]
    copies = force_ref.shape[0] // out_ref.shape[0]
    for j in range(out_ref.shape[0]):
        total = force_ref[senders[j * copies], 0:used, :]
        for c in range(1, copies):
            total += force_ref[senders[j * copies + c], 0:used, :]
        out_ref[j, 0:used, :] = total


def expand_kernel(table_ref, kept_ref, taken_ref, out_to, work_ref, out_ref, sems):
    beads = out_ref.shape[1]
    tiles = out_ref.shape[2] // LANES
    used = 3 * tiles
    stride = work_ref.shape[0] // beads
    table = table_ref[...]
    done = 0
    moves = []
    for r in range(0, used, 8):
        size = min(8, used - r)
        parts = [
            source[j, r : r + size, :] for source in (kept_ref, taken_ref) for j in range(CONTR // 2)
        ]
        for b in range(beads):
            at = b * CONTR
            total = parts[0] * table[at : at + 1]
            for j in range(1, CONTR):
                total += parts[j] * table[at + j : at + j + 1]
            work_ref[b * stride + r : b * stride + r + size, :] = total
        for i in range(r, r + size):
            x, t = divmod(i, tiles)
            out_ref[x, :, t * LANES : (t + 1) * LANES] = work_ref[
                pl.ds(i, beads, stride=stride), :
            ]
        while done < 3 and (done + 1) * tiles <= r + size:
            moves.append(pltpu.make_async_copy(out_ref.at[done], out_to.at[done], sems.at[done]))
            moves[-1].start()
            done += 1
    for move in moves:
        move.wait()


VMEM = pl.BlockSpec(memory_space=pltpu.VMEM)
HBM = pl.BlockSpec(memory_space=pltpu.HBM)
PARAMS = pltpu.CompilerParams(vmem_limit_bytes=24 * 1024 * 1024)


ORDERS = {"spots": 5, "factors": 5, "forces": 5}


def members(key):
    return [place ^ ORDERS[key] for place in range(8)]


def between_chips(array, key):
    groups = [[2 * chip + core for chip in members(key)] for core in range(2)]
    return lax.all_to_all(array, "bead", 0, 0, axis_index_groups=groups, tiled=True)


def between_cores(array):
    peers = lax.axis_size("bead")
    return lax.ppermute(array, "bead", [(i, i ^ 1) for i in range(peers)])


def shaped(*shape, dtype=jnp.float32):
    return jax.ShapeDtypeStruct(shape, dtype)


def local(points, waves, labels, species):
    beads, _, sites = points.shape
    bead_peers = lax.axis_size("bead")
    atom_peers = lax.axis_size("atom")
    tiles = sites // LANES
    used = 3 * tiles
    rows = -(-(used + 3) // 8) * 8
    sent = -(-(used + 6) // 8) * 8
    held = -(-used // 8) * 8
    half = CONTR // 2
    chips = bead_peers // 2
    beads_all = beads * bead_peers
    kept, given, charge, table = pl.pallas_call(
        functools.partial(contract_kernel, beads_all),
        out_shape=[
            shaped(half, rows, LANES),
            shaped(half, rows, LANES),
            shaped(tiles, LANES),
            shaped(beads * CONTR, LANES),
        ],
        in_specs=[HBM] * 4,
        out_specs=[VMEM] * 4,
        scratch_shapes=[
            pltpu.VMEM((used * CONTR, LANES), jnp.float32),
            pltpu.VMEM((3, beads, sites), jnp.float32),
            pltpu.VMEM(waves.shape, jnp.int32),
            pltpu.VMEM((tiles, LANES), jnp.int32),
            pltpu.VMEM((1, species.shape[0]), jnp.float32),
            pltpu.SemaphoreType.DMA((6,)),
        ],
        compiler_params=PARAMS,
        name="contract",
    )(
        *(
            pltpu.with_memory_space_constraint(a, pltpu.HBM)
            for a in (
                points.transpose(1, 0, 2),
                waves,
                labels.reshape(tiles, LANES),
                species[None, :],
            )
        )
    )
    portion = pl.pallas_call(
        functools.partial(pair_sum_kernel, used),
        out_shape=shaped(chips, sent, LANES),
        in_specs=[VMEM] * 2,
        out_specs=VMEM,
        compiler_params=PARAMS,
        name="pair_sum",
    )(kept, between_cores(given))
    spots = between_chips(portion, "spots")
    partial, weights, high, low, plain = pl.pallas_call(
        functools.partial(structure_kernel, float(sites * atom_peers)),
        out_shape=[
            shaped(atom_peers, 2 * SENT, 2 * LANES),
            shaped(2 * ROWS, LANES),
            shaped(2 * LANES, sites, dtype=jnp.bfloat16),
            shaped(2 * LANES, sites, dtype=jnp.bfloat16),
            shaped(2 * ROWS, sites),
        ],
        in_specs=[VMEM] * 2,
        out_specs=[VMEM] * 5,
        scratch_shapes=[pltpu.VMEM((4 * ROWS, sites), jnp.bfloat16)],
        compiler_params=PARAMS,
        name="structure",
    )(spots, charge)
    factors = lax.all_to_all(
        partial, "atom", 0, 0, axis_index_groups=[members("factors")], tiled=True
    )
    force = pl.pallas_call(
        force_kernel,
        out_shape=shaped(chips, held, LANES),
        in_specs=[VMEM] * 5,
        out_specs=VMEM,
        scratch_shapes=[
            pltpu.VMEM((6 * ROWS, 2 * LANES), jnp.float32),
            pltpu.VMEM((used, LANES), jnp.float32),
        ],
        compiler_params=PARAMS,
        name="force",
    )(factors, weights, high, low, plain)
    gathered = pl.pallas_call(
        functools.partial(gather_kernel, used),
        out_shape=shaped(half, held, LANES),
        in_specs=[VMEM],
        out_specs=VMEM,
        compiler_params=PARAMS,
        name="gather",
    )(between_chips(force, "forces"))
    out = pl.pallas_call(
        expand_kernel,
        out_shape=shaped(3, beads, sites),
        in_specs=[VMEM] * 3,
        out_specs=HBM,
        scratch_shapes=[
            pltpu.VMEM((beads * held, LANES), jnp.float32),
            pltpu.VMEM((3, beads, sites), jnp.float32),
            pltpu.SemaphoreType.DMA((3,)),
        ],
        compiler_params=PARAMS,
        name="expand",
    )(table, gathered, between_cores(gathered))
    return out.transpose(1, 0, 2)


def solution(mesh):
    in_specs = (P("bead", None, "atom"), P(None, "bead"), P("atom"), P())
    out_specs = P("bead", None, "atom")
    return jax.shard_map(local, mesh=mesh, in_specs=in_specs, out_specs=out_specs, check_vma=False)
```

```python
import functools
import math

import jax
import jax.numpy as jnp
import numpy as np
from jax import lax
from jax.experimental import pallas as pl
from jax.experimental.pallas import tpu as pltpu
from jax.sharding import PartitionSpec as P

CONTR = 8
LANES = 128
ROWS = 16
SENT = 12
TWO_PI = 2.0 * math.pi


def polynomials():
    nodes = 0.5 * np.cos(np.pi * (np.arange(400) + 0.5) / 400)
    u = nodes * nodes
    odd = np.linalg.lstsq(
        nodes[:, None] * u[:, None] ** np.arange(6), np.sin(2 * np.pi * nodes), rcond=None
    )[0]
    even = np.linalg.lstsq(u[:, None] ** np.arange(7), np.cos(2 * np.pi * nodes), rcond=None)[0]
    return [float(c) for c in odd], [float(c) for c in even]


ODD, EVEN = polynomials()


def horner(u, coefficients):
    total = coefficients[-1]
    for c in coefficients[-2::-1]:
        total = total * u + c
    return total


def reduced(t):
    return t - jnp.round(t)


def sin_turns(t):
    t = reduced(t)
    return t * horner(t * t, ODD)


def cos_turns(t):
    t = reduced(t)
    return horner(t * t, EVEN)


def both_turns(t):
    t = reduced(t)
    u = t * t
    return horner(u, EVEN), t * horner(u, ODD)


def iota(shape, dim):
    return lax.broadcasted_iota(jnp.int32, shape, dim).astype(jnp.float32)


def pair_of(index, core):
    tile = jnp.floor(index * 0.125)
    place = index - 8.0 * tile
    run = jnp.floor((tile + 0.5) * 0.2)
    m2 = tile - 5.0 * run + 1.0 + 5.0 * core
    last = run > 2.5
    m2 = jnp.where(last, 0.0, m2)
    run = jnp.where(last, core, run)
    return m2, run_member(run, place)


def run_member(run, place):
    middle = jnp.where(place < 0.5, 0.0, jnp.where(place < 2.5, place + 8.0, -6.0 - place))
    return jnp.where(run < 0.5, place + 1.0, jnp.where(run < 1.5, middle, -1.0 - place))


def place_of(m2, m3, core):
    size = jnp.abs(m3)
    middle = (size > 8.5) | (size < 0.5)
    run = jnp.where(middle, 1.0, jnp.where(m3 < 0, 2.0, 0.0))
    inner = jnp.where(m3 < 0, size - 6.0, jnp.maximum(size - 8.0, 0.0))
    place = jnp.where(middle, inner, size - 1.0)
    step = m2 - 1.0 - 5.0 * core
    row = (run * 5.0 + step) * 8.0 + place
    row = jnp.where((step >= 0) & (step < 5), row, -1.0)
    return jnp.where(m2 == 0.0, jnp.where(run == core, 120.0 + place, -1.0), row)


def split(value):
    high = value.astype(jnp.bfloat16)
    low = (value - high.astype(jnp.float32)).astype(jnp.bfloat16)
    return high, low


def dot_nt(a, b):
    return lax.dot_general(a, b, (((1,), (1,)), ((), ())), preferred_element_type=jnp.float32)


def table_value(bead, contracted, beads):
    turn = bead * (1.0 / beads) - contracted * (1.0 / CONTR)
    total = 1.0 + math.sqrt(2.0) * cos_turns(turn * (CONTR // 2))
    for mode in range(1, CONTR // 2):
        total += 2.0 * cos_turns(turn * mode)
    return total * (1.0 / beads)


def contract_kernel(
    beads_all,
    points_from,
    waves_from,
    labels_from,
    species_from,
    kept_ref,
    given_ref,
    charge_ref,
    table_ref,
    work_ref,
    points_ref,
    waves_ref,
    labels_ref,
    species_ref,
    sems,
):
    copies_in = [
        pltpu.make_async_copy(points_from.at[x], points_ref.at[x], sems.at[x]) for x in range(3)
    ]
    for i, (source, target) in enumerate(
        ((waves_from, waves_ref), (labels_from, labels_ref), (species_from, species_ref))
    ):
        copies_in.append(pltpu.make_async_copy(source, target, sems.at[3 + i]))
    for copy in copies_in:
        copy.start()
    beads = points_ref.shape[1]
    tiles = points_ref.shape[2] // LANES
    bead_index = lax.axis_index("bead")
    first = (bead_index * beads).astype(jnp.float32)
    start = (lax.rem(bead_index, 2) * (CONTR // 2)).astype(jnp.float32)
    columns = [
        table_value(first + b, iota((CONTR, LANES), 0) + start, beads_all) for b in range(beads)
    ]
    for b in range(beads):
        table_ref[b * CONTR : (b + 1) * CONTR, :] = columns[b]
    for x in range(3):
        copies_in[x].wait()
        for t in range(tiles):
            block = points_ref[x, :, t * LANES : (t + 1) * LANES]
            total = columns[0] * jnp.broadcast_to(block[0:1], (CONTR, LANES))
            for b in range(1, beads):
                total += columns[b] * jnp.broadcast_to(block[b : b + 1], (CONTR, LANES))
            row = (x * tiles + t) * CONTR
            work_ref[row : row + CONTR, :] = total
    used = 3 * tiles
    half = CONTR // 2
    for target, begin in ((given_ref, half), (kept_ref, 0)):
        for j in range(half):
            target[j, 0:used, :] = work_ref[pl.ds(begin + j, used, stride=CONTR), :]
    for copy in copies_in[3:]:
        copy.wait()
    waves = waves_ref[...].astype(jnp.float32)
    for target in (given_ref, kept_ref):
        target[0, used : used + 3, :] = waves
    labels = labels_ref[...]
    charge = jnp.zeros(labels.shape, jnp.float32)
    for kind in range(species_ref.shape[1]):
        value = jnp.broadcast_to(species_ref[:, kind : kind + 1], labels.shape)
        charge += jnp.where(labels == kind, value, 0.0)
    charge_ref[...] = charge


def pair_sum_kernel(used, kept_ref, taken_ref, out_ref):
    copies = out_ref.shape[0] // kept_ref.shape[0]
    kept_waves = kept_ref[0, used : used + 3, :]
    taken_waves = taken_ref[0, used : used + 3, :]
    for j in range(kept_ref.shape[0]):
        total = kept_ref[j, 0:used, :] + taken_ref[j, 0:used, :]
        for c in range(copies):
            out_ref[j * copies + c, 0:used, :] = total
            out_ref[j * copies + c, used : used + 3, :] = kept_waves
            out_ref[j * copies + c, used + 3 : used + 6, :] = taken_waves


def own_half():
    first = ORDERS["spots"]
    bit = lax.rem(lax.div(lax.axis_index("bead"), 2) + first % 2, 2)
    return bit.astype(jnp.float32)


def structure_kernel(
    number_points,
    spots_ref,
    charge_ref,
    partial_ref,
    weights_ref,
    high_ref,
    low_ref,
    plain_ref,
    charged_ref,
):
    half = own_half()
    peers = spots_ref.shape[0]
    tiles = charge_ref.shape[0]
    used = 3 * tiles
    spots = spots_ref[0, 0:used, :]
    for p in range(1, peers):
        spots += spots_ref[p, 0:used, :]
    spots = reduced(spots)
    charge = charge_ref[...]
    grid_row = iota((2 * ROWS, LANES), 0)
    back = grid_row >= ROWS
    size = jnp.where(back, grid_row - ROWS, grid_row)
    wanted = jnp.where(back, jnp.where(size > 0, -size, 1000.0), size)
    pair_row = iota((LANES, LANES), 0).astype(jnp.bfloat16)
    wanted = wanted.astype(jnp.bfloat16)
    one, zero = jnp.bfloat16(1.0), jnp.bfloat16(0.0)
    m1, m2, m3 = (
        jnp.concatenate([spots_ref[:, used + x, :], spots_ref[:, used + 3 + x, :]], axis=0)
        for x in range(3)
    )
    sign = jnp.where(m2 < 0, -1.0, 1.0)
    sign = jnp.where((m2 == 0) & (m3 < 0), -1.0, sign)
    m1 = (m1 * sign).astype(jnp.bfloat16)
    place = place_of(m2 * sign, m3 * sign, half).astype(jnp.bfloat16)
    counts = jnp.zeros((2 * ROWS, LANES), jnp.float32)
    for p in range(2 * peers):
        left = jnp.where(wanted == m1[p : p + 1], one, zero)
        right = jnp.where(pair_row == place[p : p + 1], one, zero)
        counts += dot_nt(left, right)
    m2, m3 = pair_of(iota((2 * ROWS, LANES), 1), half)
    square = size * size + m2 * m2 + m3 * m3
    square = jnp.maximum(square, 1.0)
    weights_ref[...] = counts * (4.0 * jnp.exp(square * -0.01) / (square * number_points))
    size = iota((ROWS, LANES), 0)
    steps = 1.0 + 5.0 * half + iota((8, LANES), 0)
    place = iota((8, LANES), 0)
    outer, middle = (run_member(jnp.full((8, LANES), run), place) for run in (0.0, 1.0))
    for t in range(tiles):
        lanes = slice(t * LANES, (t + 1) * LANES)
        x1 = spots[t : t + 1, :]
        x2 = spots[tiles + t : tiles + t + 1, :]
        x3 = spots[2 * tiles + t : 2 * tiles + t + 1, :]
        q = charge[t : t + 1, :]
        for index, value in enumerate(both_turns(size * x1)):
            value = q * value
            at = index * ROWS
            plain_ref[at : at + ROWS, lanes] = value
            high, low = split(value)
            charged_ref[at : at + ROWS, lanes] = high
            charged_ref[2 * ROWS + at : 3 * ROWS + at, lanes] = low
        cos2, sin2 = both_turns(steps * x2)
        cos3, sin3 = both_turns(outer * x3)
        cos4, sin4 = both_turns(middle * x3)
        cosines, sines = [None] * 15, [None] * 15
        for i in range(5):
            c2 = jnp.broadcast_to(cos2[i : i + 1], (8, LANES))
            s2 = jnp.broadcast_to(sin2[i : i + 1], (8, LANES))
            cc, ss, sc, cs = c2 * cos3, s2 * sin3, s2 * cos3, c2 * sin3
            cosines[i], sines[i] = cc - ss, sc + cs
            cosines[5 + i], sines[5 + i] = c2 * cos4 - s2 * sin4, s2 * cos4 + c2 * sin4
            cosines[10 + i], sines[10 + i] = cc + ss, sc - cs
        cosines.append(jnp.where(half == 0.0, cos3, cos4))
        sines.append(jnp.where(half == 0.0, sin3, sin4))
        for index, values in enumerate((cosines, sines)):
            for r in range(0, 16, 2):
                high, low = split(jnp.concatenate(values[r : r + 2], axis=0))
                at = index * LANES + r * 8
                high_ref[at : at + 16, lanes] = high
                low_ref[at : at + 16, lanes] = low
    total = dot_nt(charged_ref[...], high_ref[...])
    total = (
        total[0 : 2 * ROWS]
        + total[2 * ROWS :]
        + dot_nt(charged_ref[0 : 2 * ROWS, :], low_ref[...])
    )
    for p in range(partial_ref.shape[0]):
        partial_ref[p, 0:SENT, :] = total[0:SENT]
        partial_ref[p, SENT:, :] = total[ROWS : ROWS + SENT]


def force_kernel(
    partial_ref, weights_ref, high_ref, low_ref, plain_ref, out_ref, coef_ref, term_ref
):
    half = own_half()
    tiles = plain_ref.shape[1] // LANES
    cos_row = partial_ref[0, 0:SENT, :]
    sin_row = partial_ref[0, SENT:, :]
    for p in range(1, partial_ref.shape[0]):
        cos_row += partial_ref[p, 0:SENT, :]
        sin_row += partial_ref[p, SENT:, :]
    ahead = weights_ref[0:SENT, :]
    back = weights_ref[ROWS : ROWS + SENT, :]
    cc, cs = cos_row[:, :LANES], cos_row[:, LANES:]
    sc, ss = sin_row[:, :LANES], sin_row[:, LANES:]
    ahead_cos, ahead_sin = ahead * (cc - ss), ahead * (cs + sc)
    back_cos, back_sin = back * (cc + ss), back * (cs - sc)
    m2, m3 = pair_of(iota((SENT, LANES), 1), half)
    coef_ref[...] = jnp.zeros_like(coef_ref)
    rows = (
        (ahead_cos + back_cos, ahead_sin + back_sin),
        (ahead_sin - back_sin, back_cos - ahead_cos),
    )
    m1 = TWO_PI * iota((SENT, LANES), 0)
    for kind, (on_cos, on_sin) in enumerate(rows):
        at = (1 - kind) * ROWS
        along = m1 if kind == 0 else -m1
        coef_ref[at : at + SENT, :LANES] = along * on_cos
        coef_ref[at : at + SENT, LANES:] = along * on_sin
        for axis, m in enumerate((m2, m3)):
            at = kind * ROWS + 2 * ROWS * (axis + 1)
            coef_ref[at : at + SENT, :LANES] = (-TWO_PI) * m * on_sin
            coef_ref[at : at + SENT, LANES:] = TWO_PI * m * on_cos
    high, low = split(coef_ref[...])
    both = jnp.concatenate([high, low], axis=0)
    size = high.shape[0]
    width = 2 * LANES
    for t in range(0, tiles, 2):
        lanes = slice(t * LANES, t * LANES + width)
        near = jnp.dot(both, high_ref[:, lanes], preferred_element_type=jnp.float32)
        far = jnp.dot(high, low_ref[:, lanes], preferred_element_type=jnp.float32)
        term = near[:size] + near[size:] + far
        plain = plain_ref[:, lanes]
        for x in range(3):
            at = 2 * ROWS * x
            total = jnp.sum(term[at : at + 2 * ROWS] * plain, axis=0, keepdims=True)
            for i in range(2):
                term_ref[x * tiles + t + i : x * tiles + t + i + 1, :] = total[
                    :, i * LANES : (i + 1) * LANES
                ]
    block = term_ref[...]
    for p in range(out_ref.shape[0]):
        out_ref[p, 0 : block.shape[0], :] = block


def gather_kernel(used, force_ref, out_ref):
    arrivals = members("forces")
    senders = [arrivals.index(member) for member in members("spots")]
    copies = force_ref.shape[0] // out_ref.shape[0]
    for j in range(out_ref.shape[0]):
        total = force_ref[senders[j * copies], 0:used, :]
        for c in range(1, copies):
            total += force_ref[senders[j * copies + c], 0:used, :]
        out_ref[j, 0:used, :] = total


def expand_kernel(table_ref, kept_ref, taken_ref, out_to, work_ref, out_ref, sems):
    beads = out_ref.shape[1]
    tiles = out_ref.shape[2] // LANES
    used = 3 * tiles
    stride = work_ref.shape[0] // beads
    table = table_ref[...]
    done = 0
    moves = []
    for r in range(0, used, 8):
        size = min(8, used - r)
        parts = [
            source[j, r : r + size, :] for source in (kept_ref, taken_ref) for j in range(CONTR // 2)
        ]
        for b in range(beads):
            at = b * CONTR
            total = parts[0] * table[at : at + 1]
            for j in range(1, CONTR):
                total += parts[j] * table[at + j : at + j + 1]
            work_ref[b * stride + r : b * stride + r + size, :] = total
        for i in range(r, r + size):
            x, t = divmod(i, tiles)
            out_ref[x, :, t * LANES : (t + 1) * LANES] = work_ref[
                pl.ds(i, beads, stride=stride), :
            ]
        while done < 3 and (done + 1) * tiles <= r + size:
            moves.append(pltpu.make_async_copy(out_ref.at[done], out_to.at[done], sems.at[done]))
            moves[-1].start()
            done += 1
    for move in moves:
        move.wait()


VMEM = pl.BlockSpec(memory_space=pltpu.VMEM)
HBM = pl.BlockSpec(memory_space=pltpu.HBM)
PARAMS = pltpu.CompilerParams(vmem_limit_bytes=24 * 1024 * 1024)


ORDERS = {"spots": 5, "factors": 5, "forces": 5}


def members(key):
    return [place ^ ORDERS[key] for place in range(8)]


def between_chips(array, key):
    groups = [[2 * chip + core for chip in members(key)] for core in range(2)]
    return lax.all_to_all(array, "bead", 0, 0, axis_index_groups=groups, tiled=True)


def between_cores(array):
    peers = lax.axis_size("bead")
    return lax.ppermute(array, "bead", [(i, i ^ 1) for i in range(peers)])


def shaped(*shape, dtype=jnp.float32):
    return jax.ShapeDtypeStruct(shape, dtype)


def local(points, waves, labels, species):
    beads, _, sites = points.shape
    bead_peers = lax.axis_size("bead")
    atom_peers = lax.axis_size("atom")
    tiles = sites // LANES
    used = 3 * tiles
    rows = -(-(used + 3) // 8) * 8
    sent = -(-(used + 6) // 8) * 8
    held = -(-used // 8) * 8
    half = CONTR // 2
    chips = bead_peers // 2
    beads_all = beads * bead_peers
    kept, given, charge, table = pl.pallas_call(
        functools.partial(contract_kernel, beads_all),
        out_shape=[
            shaped(half, rows, LANES),
            shaped(half, rows, LANES),
            shaped(tiles, LANES),
            shaped(beads * CONTR, LANES),
        ],
        in_specs=[HBM] * 4,
        out_specs=[VMEM] * 4,
        scratch_shapes=[
            pltpu.VMEM((used * CONTR, LANES), jnp.float32),
            pltpu.VMEM((3, beads, sites), jnp.float32),
            pltpu.VMEM(waves.shape, jnp.int32),
            pltpu.VMEM((tiles, LANES), jnp.int32),
            pltpu.VMEM((1, species.shape[0]), jnp.float32),
            pltpu.SemaphoreType.DMA((6,)),
        ],
        compiler_params=PARAMS,
        name="contract",
    )(
        *(
            pltpu.with_memory_space_constraint(a, pltpu.HBM)
            for a in (
                points.transpose(1, 0, 2),
                waves,
                labels.reshape(tiles, LANES),
                species[None, :],
            )
        )
    )
    portion = pl.pallas_call(
        functools.partial(pair_sum_kernel, used),
        out_shape=shaped(chips, sent, LANES),
        in_specs=[VMEM] * 2,
        out_specs=VMEM,
        compiler_params=PARAMS,
        name="pair_sum",
    )(kept, between_cores(given))
    spots = between_chips(portion, "spots")
    partial, weights, high, low, plain = pl.pallas_call(
        functools.partial(structure_kernel, float(sites * atom_peers)),
        out_shape=[
            shaped(atom_peers, 2 * SENT, 2 * LANES),
            shaped(2 * ROWS, LANES),
            shaped(2 * LANES, sites, dtype=jnp.bfloat16),
            shaped(2 * LANES, sites, dtype=jnp.bfloat16),
            shaped(2 * ROWS, sites),
        ],
        in_specs=[VMEM] * 2,
        out_specs=[VMEM] * 5,
        scratch_shapes=[pltpu.VMEM((4 * ROWS, sites), jnp.bfloat16)],
        compiler_params=PARAMS,
        name="structure",
    )(spots, charge)
    factors = lax.all_to_all(
        partial, "atom", 0, 0, axis_index_groups=[members("factors")], tiled=True
    )
    force = pl.pallas_call(
        force_kernel,
        out_shape=shaped(chips, held, LANES),
        in_specs=[VMEM] * 5,
        out_specs=VMEM,
        scratch_shapes=[
            pltpu.VMEM((6 * ROWS, 2 * LANES), jnp.float32),
            pltpu.VMEM((used, LANES), jnp.float32),
        ],
        compiler_params=PARAMS,
        name="force",
    )(factors, weights, high, low, plain)
    gathered = pl.pallas_call(
        functools.partial(gather_kernel, used),
        out_shape=shaped(half, held, LANES),
        in_specs=[VMEM],
        out_specs=VMEM,
        compiler_params=PARAMS,
        name="gather",
    )(between_chips(force, "forces"))
    out = pl.pallas_call(
        expand_kernel,
        out_shape=shaped(3, beads, sites),
        in_specs=[VMEM] * 3,
        out_specs=HBM,
        scratch_shapes=[
            pltpu.VMEM((beads * held, LANES), jnp.float32),
            pltpu.VMEM((3, beads, sites), jnp.float32),
            pltpu.SemaphoreType.DMA((3,)),
        ],
        compiler_params=PARAMS,
        name="expand",
    )(table, gathered, between_cores(gathered))
    return out.transpose(1, 0, 2)


def solution(mesh):
    in_specs = (P("bead", None, "atom"), P(None, "bead"), P("atom"), P())
    out_specs = P("bead", None, "atom")
    return jax.shard_map(local, mesh=mesh, in_specs=in_specs, out_specs=out_specs, check_vma=False)
```

```python
import functools
import math

import jax
import jax.numpy as jnp
import numpy as np
from jax import lax
from jax.experimental import pallas as pl
from jax.experimental.pallas import tpu as pltpu
from jax.sharding import PartitionSpec as P

CONTR = 8
LANES = 128
ROWS = 16
SENT = 12
TWO_PI = 2.0 * math.pi


def polynomials():
    nodes = 0.5 * np.cos(np.pi * (np.arange(400) + 0.5) / 400)
    u = nodes * nodes
    odd = np.linalg.lstsq(
        nodes[:, None] * u[:, None] ** np.arange(6), np.sin(2 * np.pi * nodes), rcond=None
    )[0]
    even = np.linalg.lstsq(u[:, None] ** np.arange(7), np.cos(2 * np.pi * nodes), rcond=None)[0]
    return [float(c) for c in odd], [float(c) for c in even]


ODD, EVEN = polynomials()


def horner(u, coefficients):
    total = coefficients[-1]
    for c in coefficients[-2::-1]:
        total = total * u + c
    return total


def reduced(t):
    return t - jnp.round(t)


def sin_turns(t):
    t = reduced(t)
    return t * horner(t * t, ODD)


def cos_turns(t):
    t = reduced(t)
    return horner(t * t, EVEN)


def both_turns(t):
    t = reduced(t)
    u = t * t
    return horner(u, EVEN), t * horner(u, ODD)


def iota(shape, dim):
    return lax.broadcasted_iota(jnp.int32, shape, dim).astype(jnp.float32)


def pair_of(index, core):
    tile = jnp.floor(index * 0.125)
    place = index - 8.0 * tile
    run = jnp.floor((tile + 0.5) * 0.2)
    m2 = tile - 5.0 * run + 1.0 + 5.0 * core
    last = run > 2.5
    m2 = jnp.where(last, 0.0, m2)
    run = jnp.where(last, core, run)
    return m2, run_member(run, place)


def run_member(run, place):
    middle = jnp.where(place < 0.5, 0.0, jnp.where(place < 2.5, place + 8.0, -6.0 - place))
    return jnp.where(run < 0.5, place + 1.0, jnp.where(run < 1.5, middle, -1.0 - place))


def place_of(m2, m3, core):
    size = jnp.abs(m3)
    middle = (size > 8.5) | (size < 0.5)
    run = jnp.where(middle, 1.0, jnp.where(m3 < 0, 2.0, 0.0))
    inner = jnp.where(m3 < 0, size - 6.0, jnp.maximum(size - 8.0, 0.0))
    place = jnp.where(middle, inner, size - 1.0)
    step = m2 - 1.0 - 5.0 * core
    row = (run * 5.0 + step) * 8.0 + place
    row = jnp.where((step >= 0) & (step < 5), row, -1.0)
    return jnp.where(m2 == 0.0, jnp.where(run == core, 120.0 + place, -1.0), row)


def split(value):
    high = value.astype(jnp.bfloat16)
    low = (value - high.astype(jnp.float32)).astype(jnp.bfloat16)
    return high, low


def dot_nt(a, b):
    return lax.dot_general(a, b, (((1,), (1,)), ((), ())), preferred_element_type=jnp.float32)


def table_value(bead, contracted, beads):
    turn = bead * (1.0 / beads) - contracted * (1.0 / CONTR)
    total = 1.0 + math.sqrt(2.0) * cos_turns(turn * (CONTR // 2))
    for mode in range(1, CONTR // 2):
        total += 2.0 * cos_turns(turn * mode)
    return total * (1.0 / beads)


def contract_kernel(
    beads_all,
    points_from,
    waves_from,
    labels_from,
    species_from,
    kept_ref,
    given_ref,
    charge_ref,
    table_ref,
    work_ref,
    points_ref,
    waves_ref,
    labels_ref,
    species_ref,
    sems,
):
    copies_in = [
        pltpu.make_async_copy(points_from.at[x], points_ref.at[x], sems.at[x]) for x in range(3)
    ]
    for i, (source, target) in enumerate(
        ((waves_from, waves_ref), (labels_from, labels_ref), (species_from, species_ref))
    ):
        copies_in.append(pltpu.make_async_copy(source, target, sems.at[3 + i]))
    for copy in copies_in:
        copy.start()
    beads = points_ref.shape[1]
    tiles = points_ref.shape[2] // LANES
    bead_index = lax.axis_index("bead")
    first = (bead_index * beads).astype(jnp.float32)
    flip = flipped(lax.div(bead_index, 2))
    start = (lax.rem(bead_index + flip, 2) * (CONTR // 2)).astype(jnp.float32)
    columns = [
        table_value(first + b, iota((CONTR, LANES), 0) + start, beads_all) for b in range(beads)
    ]
    for b in range(beads):
        table_ref[b * CONTR : (b + 1) * CONTR, :] = columns[b]
    for x in range(3):
        copies_in[x].wait()
        for t in range(tiles):
            block = points_ref[x, :, t * LANES : (t + 1) * LANES]
            total = columns[0] * jnp.broadcast_to(block[0:1], (CONTR, LANES))
            for b in range(1, beads):
                total += columns[b] * jnp.broadcast_to(block[b : b + 1], (CONTR, LANES))
            row = (x * tiles + t) * CONTR
            work_ref[row : row + CONTR, :] = total
    used = 3 * tiles
    half = CONTR // 2
    for target, begin in ((given_ref, half), (kept_ref, 0)):
        for j in range(half):
            target[j, 0:used, :] = work_ref[pl.ds(begin + j, used, stride=CONTR), :]
    for copy in copies_in[3:]:
        copy.wait()
    waves = waves_ref[...].astype(jnp.float32)
    for target in (given_ref, kept_ref):
        target[0, used : used + 3, :] = waves
    labels = labels_ref[...]
    charge = jnp.zeros(labels.shape, jnp.float32)
    for kind in range(species_ref.shape[1]):
        value = jnp.broadcast_to(species_ref[:, kind : kind + 1], labels.shape)
        charge += jnp.where(labels == kind, value, 0.0)
    charge_ref[...] = charge


def pair_sum_kernel(used, kept_ref, taken_ref, out_ref):
    copies = out_ref.shape[0] // kept_ref.shape[0]
    kept_waves = kept_ref[0, used : used + 3, :]
    taken_waves = taken_ref[0, used : used + 3, :]
    for j in range(kept_ref.shape[0]):
        total = kept_ref[j, 0:used, :] + taken_ref[j, 0:used, :]
        for c in range(copies):
            out_ref[j * copies + c, 0:used, :] = total
            out_ref[j * copies + c, used : used + 3, :] = kept_waves
            out_ref[j * copies + c, used + 3 : used + 6, :] = taken_waves


def members(key):
    return [place ^ FIRST[key] for place in range(8)]


def own_half():
    first = FIRST["spots"]
    bit = lax.rem(lax.div(lax.axis_index("bead"), 2) + first % 2, 2)
    return bit.astype(jnp.float32)


def structure_kernel(
    number_points,
    spots_ref,
    charge_ref,
    partial_ref,
    weights_ref,
    high_ref,
    low_ref,
    plain_ref,
    charged_ref,
):
    half = own_half()
    peers = spots_ref.shape[0]
    tiles = charge_ref.shape[0]
    used = 3 * tiles
    spots = spots_ref[0, 0:used, :]
    for p in range(1, peers):
        spots += spots_ref[p, 0:used, :]
    spots = reduced(spots)
    charge = charge_ref[...]
    grid_row = iota((2 * ROWS, LANES), 0)
    back = grid_row >= ROWS
    size = jnp.where(back, grid_row - ROWS, grid_row)
    wanted = jnp.where(back, jnp.where(size > 0, -size, 1000.0), size)
    pair_row = iota((LANES, LANES), 0).astype(jnp.bfloat16)
    wanted = wanted.astype(jnp.bfloat16)
    one, zero = jnp.bfloat16(1.0), jnp.bfloat16(0.0)
    m1, m2, m3 = (
        jnp.concatenate([spots_ref[:, used + x, :], spots_ref[:, used + 3 + x, :]], axis=0)
        for x in range(3)
    )
    sign = jnp.where(m2 < 0, -1.0, 1.0)
    sign = jnp.where((m2 == 0) & (m3 < 0), -1.0, sign)
    m1 = (m1 * sign).astype(jnp.bfloat16)
    place = place_of(m2 * sign, m3 * sign, half).astype(jnp.bfloat16)
    counts = jnp.zeros((2 * ROWS, LANES), jnp.float32)
    for p in range(2 * peers):
        left = jnp.where(wanted == m1[p : p + 1], one, zero)
        right = jnp.where(pair_row == place[p : p + 1], one, zero)
        counts += dot_nt(left, right)
    m2, m3 = pair_of(iota((2 * ROWS, LANES), 1), half)
    square = size * size + m2 * m2 + m3 * m3
    square = jnp.maximum(square, 1.0)
    weights_ref[...] = counts * (4.0 * jnp.exp(square * -0.01) / (square * number_points))
    size = iota((ROWS, LANES), 0)
    steps = 1.0 + 5.0 * half + iota((8, LANES), 0)
    place = iota((8, LANES), 0)
    outer, middle = (run_member(jnp.full((8, LANES), run), place) for run in (0.0, 1.0))
    for t in range(tiles):
        lanes = slice(t * LANES, (t + 1) * LANES)
        x1 = spots[t : t + 1, :]
        x2 = spots[tiles + t : tiles + t + 1, :]
        x3 = spots[2 * tiles + t : 2 * tiles + t + 1, :]
        q = charge[t : t + 1, :]
        for index, value in enumerate(both_turns(size * x1)):
            value = q * value
            at = index * ROWS
            plain_ref[at : at + ROWS, lanes] = value
            high, low = split(value)
            charged_ref[at : at + ROWS, lanes] = high
            charged_ref[2 * ROWS + at : 3 * ROWS + at, lanes] = low
        cos2, sin2 = both_turns(steps * x2)
        cos3, sin3 = both_turns(outer * x3)
        cos4, sin4 = both_turns(middle * x3)
        cosines, sines = [None] * 15, [None] * 15
        for i in range(5):
            c2 = jnp.broadcast_to(cos2[i : i + 1], (8, LANES))
            s2 = jnp.broadcast_to(sin2[i : i + 1], (8, LANES))
            cc, ss, sc, cs = c2 * cos3, s2 * sin3, s2 * cos3, c2 * sin3
            cosines[i], sines[i] = cc - ss, sc + cs
            cosines[5 + i], sines[5 + i] = c2 * cos4 - s2 * sin4, s2 * cos4 + c2 * sin4
            cosines[10 + i], sines[10 + i] = cc + ss, sc - cs
        cosines.append(jnp.where(half == 0.0, cos3, cos4))
        sines.append(jnp.where(half == 0.0, sin3, sin4))
        for index, values in enumerate((cosines, sines)):
            for r in range(0, 16, 2):
                high, low = split(jnp.concatenate(values[r : r + 2], axis=0))
                at = index * LANES + r * 8
                high_ref[at : at + 16, lanes] = high
                low_ref[at : at + 16, lanes] = low
    total = dot_nt(charged_ref[...], high_ref[...])
    total = (
        total[0 : 2 * ROWS]
        + total[2 * ROWS :]
        + dot_nt(charged_ref[0 : 2 * ROWS, :], low_ref[...])
    )
    for p in range(partial_ref.shape[0]):
        partial_ref[p, 0:SENT, :] = total[0:SENT]
        partial_ref[p, SENT:, :] = total[ROWS : ROWS + SENT]


def force_kernel(
    partial_ref, weights_ref, high_ref, low_ref, plain_ref, out_ref, coef_ref, term_ref
):
    half = own_half()
    tiles = plain_ref.shape[1] // LANES
    cos_row = partial_ref[0, 0:SENT, :]
    sin_row = partial_ref[0, SENT:, :]
    for p in range(1, partial_ref.shape[0]):
        cos_row += partial_ref[p, 0:SENT, :]
        sin_row += partial_ref[p, SENT:, :]
    ahead = weights_ref[0:SENT, :]
    back = weights_ref[ROWS : ROWS + SENT, :]
    cc, cs = cos_row[:, :LANES], cos_row[:, LANES:]
    sc, ss = sin_row[:, :LANES], sin_row[:, LANES:]
    ahead_cos, ahead_sin = ahead * (cc - ss), ahead * (cs + sc)
    back_cos, back_sin = back * (cc + ss), back * (cs - sc)
    m2, m3 = pair_of(iota((SENT, LANES), 1), half)
    coef_ref[...] = jnp.zeros_like(coef_ref)
    rows = (
        (ahead_cos + back_cos, ahead_sin + back_sin),
        (ahead_sin - back_sin, back_cos - ahead_cos),
    )
    m1 = TWO_PI * iota((SENT, LANES), 0)
    for kind, (on_cos, on_sin) in enumerate(rows):
        at = (1 - kind) * ROWS
        along = m1 if kind == 0 else -m1
        coef_ref[at : at + SENT, :LANES] = along * on_cos
        coef_ref[at : at + SENT, LANES:] = along * on_sin
        for axis, m in enumerate((m2, m3)):
            at = kind * ROWS + 2 * ROWS * (axis + 1)
            coef_ref[at : at + SENT, :LANES] = (-TWO_PI) * m * on_sin
            coef_ref[at : at + SENT, LANES:] = TWO_PI * m * on_cos
    high, low = split(coef_ref[...])
    both = jnp.concatenate([high, low], axis=0)
    size = high.shape[0]
    width = 2 * LANES
    for t in range(0, tiles, 2):
        lanes = slice(t * LANES, t * LANES + width)
        near = jnp.dot(both, high_ref[:, lanes], preferred_element_type=jnp.float32)
        far = jnp.dot(high, low_ref[:, lanes], preferred_element_type=jnp.float32)
        term = near[:size] + near[size:] + far
        plain = plain_ref[:, lanes]
        for x in range(3):
            at = 2 * ROWS * x
            total = jnp.sum(term[at : at + 2 * ROWS] * plain, axis=0, keepdims=True)
            for i in range(2):
                term_ref[x * tiles + t + i : x * tiles + t + i + 1, :] = total[
                    :, i * LANES : (i + 1) * LANES
                ]
    block = term_ref[...]
    for p in range(out_ref.shape[0]):
        out_ref[p, 0 : block.shape[0], :] = block


def gather_kernel(used, force_ref, out_ref):
    arrivals = members("forces")
    senders = [arrivals.index(member) for member in members("spots")]
    copies = force_ref.shape[0] // out_ref.shape[0]
    for j in range(out_ref.shape[0]):
        total = force_ref[senders[j * copies], 0:used, :]
        for c in range(1, copies):
            total += force_ref[senders[j * copies + c], 0:used, :]
        out_ref[j, 0:used, :] = total


def expand_kernel(table_ref, kept_ref, taken_ref, out_to, work_ref, out_ref, sems):
    beads = out_ref.shape[1]
    tiles = out_ref.shape[2] // LANES
    used = 3 * tiles
    stride = work_ref.shape[0] // beads
    table = table_ref[...]
    done = 0
    moves = []
    for r in range(0, used, 8):
        size = min(8, used - r)
        parts = [
            source[j, r : r + size, :] for source in (kept_ref, taken_ref) for j in range(CONTR // 2)
        ]
        for b in range(beads):
            at = b * CONTR
            total = parts[0] * table[at : at + 1]
            for j in range(1, CONTR):
                total += parts[j] * table[at + j : at + j + 1]
            work_ref[b * stride + r : b * stride + r + size, :] = total
        for i in range(r, r + size):
            x, t = divmod(i, tiles)
            out_ref[x, :, t * LANES : (t + 1) * LANES] = work_ref[
                pl.ds(i, beads, stride=stride), :
            ]
        while done < 3 and (done + 1) * tiles <= r + size:
            moves.append(pltpu.make_async_copy(out_ref.at[done], out_to.at[done], sems.at[done]))
            moves[-1].start()
            done += 1
    for move in moves:
        move.wait()


VMEM = pl.BlockSpec(memory_space=pltpu.VMEM)
HBM = pl.BlockSpec(memory_space=pltpu.HBM)
PARAMS = pltpu.CompilerParams(vmem_limit_bytes=24 * 1024 * 1024)


FIRST = {"spots": 5, "factors": 5, "forces": 5}


def flipped(chip):
    return lax.div(chip, 4) if isinstance(chip, jax.Array) else chip // 4


def between(array, key):
    count = 8
    groups = []
    for side in range(2):
        for index in range(count):
            group = []
            for place in range(count):
                chip, block = place ^ FIRST[key], index
                if key == "factors":
                    chip, block = block, chip
                core = side ^ flipped(chip)
                group.append((2 * chip + core) * count + block)
            groups.append(group)
    return lax.all_to_all(
        array, ("bead", "atom"), 0, 0, axis_index_groups=groups, tiled=True
    )


def between_cores(array):
    peers = lax.axis_size("bead")
    return lax.ppermute(array, "bead", [(i, i ^ 1) for i in range(peers)])


def shaped(*shape, dtype=jnp.float32):
    return jax.ShapeDtypeStruct(shape, dtype)


def local(points, waves, labels, species):
    beads, _, sites = points.shape
    bead_peers = lax.axis_size("bead")
    atom_peers = lax.axis_size("atom")
    tiles = sites // LANES
    used = 3 * tiles
    rows = -(-(used + 3) // 8) * 8
    sent = -(-(used + 6) // 8) * 8
    held = -(-used // 8) * 8
    half = CONTR // 2
    chips = bead_peers // 2
    beads_all = beads * bead_peers
    kept, given, charge, table = pl.pallas_call(
        functools.partial(contract_kernel, beads_all),
        out_shape=[
            shaped(half, rows, LANES),
            shaped(half, rows, LANES),
            shaped(tiles, LANES),
            shaped(beads * CONTR, LANES),
        ],
        in_specs=[HBM] * 4,
        out_specs=[VMEM] * 4,
        scratch_shapes=[
            pltpu.VMEM((rows * CONTR, LANES), jnp.float32),
            pltpu.VMEM((3, beads, sites), jnp.float32),
            pltpu.VMEM(waves.shape, jnp.int32),
            pltpu.VMEM((tiles, LANES), jnp.int32),
            pltpu.VMEM((1, species.shape[0]), jnp.float32),
            pltpu.SemaphoreType.DMA((6,)),
        ],
        compiler_params=PARAMS,
        name="contract",
    )(
        *(
            pltpu.with_memory_space_constraint(a, pltpu.HBM)
            for a in (
                points.transpose(1, 0, 2),
                waves,
                labels.reshape(tiles, LANES),
                species[None, :],
            )
        )
    )
    portion = pl.pallas_call(
        functools.partial(pair_sum_kernel, used),
        out_shape=shaped(chips, sent, LANES),
        in_specs=[VMEM] * 2,
        out_specs=VMEM,
        compiler_params=PARAMS,
        name="pair_sum",
    )(kept, between_cores(given))
    spots = between(portion, "spots")
    partial, weights, high, low, plain = pl.pallas_call(
        functools.partial(structure_kernel, float(sites * atom_peers)),
        out_shape=[
            shaped(atom_peers, 2 * SENT, 2 * LANES),
            shaped(2 * ROWS, LANES),
            shaped(2 * LANES, sites, dtype=jnp.bfloat16),
            shaped(2 * LANES, sites, dtype=jnp.bfloat16),
            shaped(2 * ROWS, sites),
        ],
        in_specs=[VMEM] * 2,
        out_specs=[VMEM] * 5,
        scratch_shapes=[pltpu.VMEM((4 * ROWS, sites), jnp.bfloat16)],
        compiler_params=PARAMS,
        name="structure",
    )(spots, charge)
    factors = between(partial, "factors")
    force = pl.pallas_call(
        force_kernel,
        out_shape=shaped(chips, held, LANES),
        in_specs=[VMEM] * 5,
        out_specs=VMEM,
        scratch_shapes=[
            pltpu.VMEM((6 * ROWS, 2 * LANES), jnp.float32),
            pltpu.VMEM((used, LANES), jnp.float32),
        ],
        compiler_params=PARAMS,
        name="force",
    )(factors, weights, high, low, plain)
    gathered = pl.pallas_call(
        functools.partial(gather_kernel, used),
        out_shape=shaped(half, held, LANES),
        in_specs=[VMEM],
        out_specs=VMEM,
        compiler_params=PARAMS,
        name="gather",
    )(between(force, "forces"))
    out = pl.pallas_call(
        expand_kernel,
        out_shape=shaped(3, beads, sites),
        in_specs=[VMEM] * 3,
        out_specs=HBM,
        scratch_shapes=[
            pltpu.VMEM((beads * held, LANES), jnp.float32),
            pltpu.VMEM((3, beads, sites), jnp.float32),
            pltpu.SemaphoreType.DMA((3,)),
        ],
        compiler_params=PARAMS,
        name="expand",
    )(table, gathered, between_cores(gathered))
    return out.transpose(1, 0, 2)


def solution(mesh):
    in_specs = (P("bead", None, "atom"), P(None, "bead"), P("atom"), P())
    out_specs = P("bead", None, "atom")
    return jax.shard_map(local, mesh=mesh, in_specs=in_specs, out_specs=out_specs, check_vma=False)
```

```python
import functools
import math

import jax
import jax.numpy as jnp
import numpy as np
from jax import lax
from jax.experimental import pallas as pl
from jax.experimental.pallas import tpu as pltpu
from jax.sharding import PartitionSpec as P

CONTR = 8
LANES = 128
ROWS = 16
SENT = 12
TWO_PI = 2.0 * math.pi


def polynomials():
    nodes = 0.5 * np.cos(np.pi * (np.arange(400) + 0.5) / 400)
    u = nodes * nodes
    odd = np.linalg.lstsq(
        nodes[:, None] * u[:, None] ** np.arange(6), np.sin(2 * np.pi * nodes), rcond=None
    )[0]
    even = np.linalg.lstsq(u[:, None] ** np.arange(7), np.cos(2 * np.pi * nodes), rcond=None)[0]
    return [float(c) for c in odd], [float(c) for c in even]


ODD, EVEN = polynomials()


def horner(u, coefficients):
    total = coefficients[-1]
    for c in coefficients[-2::-1]:
        total = total * u + c
    return total


def reduced(t):
    return t - jnp.round(t)


def sin_turns(t):
    t = reduced(t)
    return t * horner(t * t, ODD)


def cos_turns(t):
    t = reduced(t)
    return horner(t * t, EVEN)


def both_turns(t):
    t = reduced(t)
    u = t * t
    return horner(u, EVEN), t * horner(u, ODD)


def iota(shape, dim):
    return lax.broadcasted_iota(jnp.int32, shape, dim).astype(jnp.float32)


def pair_of(index, core):
    tile = jnp.floor(index * 0.125)
    place = index - 8.0 * tile
    run = jnp.floor((tile + 0.5) * 0.2)
    m2 = tile - 5.0 * run + 1.0 + 5.0 * core
    last = run > 2.5
    m2 = jnp.where(last, 0.0, m2)
    run = jnp.where(last, core, run)
    return m2, run_member(run, place)


def run_member(run, place):
    middle = jnp.where(place < 0.5, 0.0, jnp.where(place < 2.5, place + 8.0, -6.0 - place))
    return jnp.where(run < 0.5, place + 1.0, jnp.where(run < 1.5, middle, -1.0 - place))


def place_of(m2, m3, core):
    size = jnp.abs(m3)
    middle = (size > 8.5) | (size < 0.5)
    run = jnp.where(middle, 1.0, jnp.where(m3 < 0, 2.0, 0.0))
    inner = jnp.where(m3 < 0, size - 6.0, jnp.maximum(size - 8.0, 0.0))
    place = jnp.where(middle, inner, size - 1.0)
    step = m2 - 1.0 - 5.0 * core
    row = (run * 5.0 + step) * 8.0 + place
    row = jnp.where((step >= 0) & (step < 5), row, -1.0)
    return jnp.where(m2 == 0.0, jnp.where(run == core, 120.0 + place, -1.0), row)


def split(value):
    high = value.astype(jnp.bfloat16)
    low = (value - high.astype(jnp.float32)).astype(jnp.bfloat16)
    return high, low


def dot_nt(a, b):
    return lax.dot_general(a, b, (((1,), (1,)), ((), ())), preferred_element_type=jnp.float32)


def table_value(bead, contracted, beads):
    turn = bead * (1.0 / beads) - contracted * (1.0 / CONTR)
    total = 1.0 + math.sqrt(2.0) * cos_turns(turn * (CONTR // 2))
    for mode in range(1, CONTR // 2):
        total += 2.0 * cos_turns(turn * mode)
    return total * (1.0 / beads)


def contract_kernel(
    beads_all,
    points_from,
    waves_from,
    labels_from,
    species_from,
    work_ref,
    given_ref,
    charge_ref,
    table_ref,
    points_ref,
    waves_ref,
    labels_ref,
    species_ref,
    sems,
):
    copies_in = [
        pltpu.make_async_copy(points_from.at[x], points_ref.at[x], sems.at[x]) for x in range(3)
    ]
    for i, (source, target) in enumerate(
        ((waves_from, waves_ref), (labels_from, labels_ref), (species_from, species_ref))
    ):
        copies_in.append(pltpu.make_async_copy(source, target, sems.at[3 + i]))
    for copy in copies_in:
        copy.start()
    beads = points_ref.shape[1]
    tiles = points_ref.shape[2] // LANES
    bead_index = lax.axis_index("bead")
    first = (bead_index * beads).astype(jnp.float32)
    flip = flipped(lax.div(bead_index, 2))
    start = (lax.rem(bead_index + flip, 2) * (CONTR // 2)).astype(jnp.float32)
    columns = [
        table_value(first + b, iota((CONTR, LANES), 0) + start, beads_all) for b in range(beads)
    ]
    for b in range(beads):
        table_ref[b * CONTR : (b + 1) * CONTR, :] = columns[b]
    for x in range(3):
        copies_in[x].wait()
        for t in range(tiles):
            block = points_ref[x, :, t * LANES : (t + 1) * LANES]
            total = columns[0] * jnp.broadcast_to(block[0:1], (CONTR, LANES))
            for b in range(1, beads):
                total += columns[b] * jnp.broadcast_to(block[b : b + 1], (CONTR, LANES))
            row = (x * tiles + t) * CONTR
            work_ref[row : row + CONTR, :] = total
    used = 3 * tiles
    half = CONTR // 2
    for j in range(half):
        given_ref[j, 0:used, :] = work_ref[pl.ds(half + j, used, stride=CONTR), :]
    for copy in copies_in[3:]:
        copy.wait()
    waves = waves_ref[...].astype(jnp.float32)
    given_ref[0, used : used + 3, :] = waves
    labels = labels_ref[...]
    charge = jnp.zeros(labels.shape, jnp.float32)
    for kind in range(species_ref.shape[1]):
        value = jnp.broadcast_to(species_ref[:, kind : kind + 1], labels.shape)
        charge += jnp.where(labels == kind, value, 0.0)
    charge_ref[...] = charge


def pair_sum_kernel(used, work_ref, given_ref, taken_ref, out_ref):
    copies = out_ref.shape[0] // given_ref.shape[0]
    kept_waves = given_ref[0, used : used + 3, :]
    taken_waves = taken_ref[0, used : used + 3, :]
    for j in range(given_ref.shape[0]):
        total = work_ref[pl.ds(j, used, stride=CONTR), :] + taken_ref[j, 0:used, :]
        for c in range(copies):
            out_ref[j * copies + c, 0:used, :] = total
            out_ref[j * copies + c, used : used + 3, :] = kept_waves
            out_ref[j * copies + c, used + 3 : used + 6, :] = taken_waves


def members(key):
    return [place ^ FIRST[key] for place in range(8)]


def own_half():
    first = FIRST["spots"]
    bit = lax.rem(lax.div(lax.axis_index("bead"), 2) + first % 2, 2)
    return bit.astype(jnp.float32)


def structure_kernel(
    number_points,
    spots_ref,
    charge_ref,
    partial_ref,
    weights_ref,
    high_ref,
    low_ref,
    plain_ref,
    charged_ref,
):
    half = own_half()
    peers = spots_ref.shape[0]
    tiles = charge_ref.shape[0]
    used = 3 * tiles
    spots = spots_ref[0, 0:used, :]
    for p in range(1, peers):
        spots += spots_ref[p, 0:used, :]
    spots = reduced(spots)
    charge = charge_ref[...]
    grid_row = iota((2 * ROWS, LANES), 0)
    back = grid_row >= ROWS
    size = jnp.where(back, grid_row - ROWS, grid_row)
    wanted = jnp.where(back, jnp.where(size > 0, -size, 1000.0), size)
    pair_row = iota((LANES, LANES), 0).astype(jnp.bfloat16)
    wanted = wanted.astype(jnp.bfloat16)
    one, zero = jnp.bfloat16(1.0), jnp.bfloat16(0.0)
    m1, m2, m3 = (
        jnp.concatenate([spots_ref[:, used + x, :], spots_ref[:, used + 3 + x, :]], axis=0)
        for x in range(3)
    )
    sign = jnp.where(m2 < 0, -1.0, 1.0)
    sign = jnp.where((m2 == 0) & (m3 < 0), -1.0, sign)
    m1 = (m1 * sign).astype(jnp.bfloat16)
    place = place_of(m2 * sign, m3 * sign, half).astype(jnp.bfloat16)
    counts = jnp.zeros((2 * ROWS, LANES), jnp.float32)
    for p in range(2 * peers):
        left = jnp.where(wanted == m1[p : p + 1], one, zero)
        right = jnp.where(pair_row == place[p : p + 1], one, zero)
        counts += dot_nt(left, right)
    m2, m3 = pair_of(iota((2 * ROWS, LANES), 1), half)
    square = size * size + m2 * m2 + m3 * m3
    square = jnp.maximum(square, 1.0)
    weights_ref[...] = counts * (4.0 * jnp.exp(square * -0.01) / (square * number_points))
    size = iota((ROWS, LANES), 0)
    steps = 1.0 + 5.0 * half + iota((8, LANES), 0)
    place = iota((8, LANES), 0)
    outer, middle = (run_member(jnp.full((8, LANES), run), place) for run in (0.0, 1.0))
    for t in range(tiles):
        lanes = slice(t * LANES, (t + 1) * LANES)
        x1 = spots[t : t + 1, :]
        x2 = spots[tiles + t : tiles + t + 1, :]
        x3 = spots[2 * tiles + t : 2 * tiles + t + 1, :]
        q = charge[t : t + 1, :]
        for index, value in enumerate(both_turns(size * x1)):
            value = q * value
            at = index * ROWS
            plain_ref[at : at + ROWS, lanes] = value
            high, low = split(value)
            charged_ref[at : at + ROWS, lanes] = high
            charged_ref[2 * ROWS + at : 3 * ROWS + at, lanes] = low
        cos2, sin2 = both_turns(steps * x2)
        cos3, sin3 = both_turns(outer * x3)
        cos4, sin4 = both_turns(middle * x3)
        cosines, sines = [None] * 15, [None] * 15
        for i in range(5):
            c2 = jnp.broadcast_to(cos2[i : i + 1], (8, LANES))
            s2 = jnp.broadcast_to(sin2[i : i + 1], (8, LANES))
            cc, ss, sc, cs = c2 * cos3, s2 * sin3, s2 * cos3, c2 * sin3
            cosines[i], sines[i] = cc - ss, sc + cs
            cosines[5 + i], sines[5 + i] = c2 * cos4 - s2 * sin4, s2 * cos4 + c2 * sin4
            cosines[10 + i], sines[10 + i] = cc + ss, sc - cs
        cosines.append(jnp.where(half == 0.0, cos3, cos4))
        sines.append(jnp.where(half == 0.0, sin3, sin4))
        for index, values in enumerate((cosines, sines)):
            for r in range(0, 16, 2):
                high, low = split(jnp.concatenate(values[r : r + 2], axis=0))
                at = index * LANES + r * 8
                high_ref[at : at + 16, lanes] = high
                low_ref[at : at + 16, lanes] = low
    total = dot_nt(charged_ref[...], high_ref[...])
    total = (
        total[0 : 2 * ROWS]
        + total[2 * ROWS :]
        + dot_nt(charged_ref[0 : 2 * ROWS, :], low_ref[...])
    )
    for p in range(partial_ref.shape[0]):
        partial_ref[p, 0:SENT, :] = total[0:SENT]
        partial_ref[p, SENT:, :] = total[ROWS : ROWS + SENT]


def force_kernel(
    partial_ref, weights_ref, high_ref, low_ref, plain_ref, out_ref, coef_ref, term_ref
):
    half = own_half()
    tiles = plain_ref.shape[1] // LANES
    cos_row = partial_ref[0, 0:SENT, :]
    sin_row = partial_ref[0, SENT:, :]
    for p in range(1, partial_ref.shape[0]):
        cos_row += partial_ref[p, 0:SENT, :]
        sin_row += partial_ref[p, SENT:, :]
    ahead = weights_ref[0:SENT, :]
    back = weights_ref[ROWS : ROWS + SENT, :]
    cc, cs = cos_row[:, :LANES], cos_row[:, LANES:]
    sc, ss = sin_row[:, :LANES], sin_row[:, LANES:]
    ahead_cos, ahead_sin = ahead * (cc - ss), ahead * (cs + sc)
    back_cos, back_sin = back * (cc + ss), back * (cs - sc)
    m2, m3 = pair_of(iota((SENT, LANES), 1), half)
    coef_ref[...] = jnp.zeros_like(coef_ref)
    rows = (
        (ahead_cos + back_cos, ahead_sin + back_sin),
        (ahead_sin - back_sin, back_cos - ahead_cos),
    )
    m1 = TWO_PI * iota((SENT, LANES), 0)
    for kind, (on_cos, on_sin) in enumerate(rows):
        at = (1 - kind) * ROWS
        along = m1 if kind == 0 else -m1
        coef_ref[at : at + SENT, :LANES] = along * on_cos
        coef_ref[at : at + SENT, LANES:] = along * on_sin
        for axis, m in enumerate((m2, m3)):
            at = kind * ROWS + 2 * ROWS * (axis + 1)
            coef_ref[at : at + SENT, :LANES] = (-TWO_PI) * m * on_sin
            coef_ref[at : at + SENT, LANES:] = TWO_PI * m * on_cos
    high, low = split(coef_ref[...])
    both = jnp.concatenate([high, low], axis=0)
    size = high.shape[0]
    width = 2 * LANES
    for t in range(0, tiles, 2):
        lanes = slice(t * LANES, t * LANES + width)
        near = jnp.dot(both, high_ref[:, lanes], preferred_element_type=jnp.float32)
        far = jnp.dot(high, low_ref[:, lanes], preferred_element_type=jnp.float32)
        term = near[:size] + near[size:] + far
        plain = plain_ref[:, lanes]
        for x in range(3):
            at = 2 * ROWS * x
            total = jnp.sum(term[at : at + 2 * ROWS] * plain, axis=0, keepdims=True)
            for i in range(2):
                term_ref[x * tiles + t + i : x * tiles + t + i + 1, :] = total[
                    :, i * LANES : (i + 1) * LANES
                ]
    block = term_ref[...]
    for p in range(out_ref.shape[0]):
        out_ref[p, 0 : block.shape[0], :] = block


def gather_kernel(used, force_ref, out_ref):
    arrivals = members("forces")
    senders = [arrivals.index(member) for member in members("spots")]
    copies = force_ref.shape[0] // out_ref.shape[0]
    for j in range(out_ref.shape[0]):
        total = force_ref[senders[j * copies], 0:used, :]
        for c in range(1, copies):
            total += force_ref[senders[j * copies + c], 0:used, :]
        out_ref[j, 0:used, :] = total


def own_kernel(used, table_ref, kept_ref, out_ref):
    parts = [kept_ref[j, 0:used, :] for j in range(kept_ref.shape[0])]
    for b in range(out_ref.shape[0]):
        at = b * CONTR
        total = parts[0] * table_ref[at : at + 1]
        for j in range(1, len(parts)):
            total += parts[j] * table_ref[at + j : at + j + 1]
        out_ref[b, 0:used, :] = total


def expand_kernel(table_ref, own_ref, taken_ref, out_to, work_ref, out_ref, sems):
    beads = out_ref.shape[1]
    tiles = out_ref.shape[2] // LANES
    used = 3 * tiles
    stride = work_ref.shape[0] // beads
    table = table_ref[...]
    done = 0
    moves = []
    for r in range(0, used, 8):
        size = min(8, used - r)
        parts = [taken_ref[j, r : r + size, :] for j in range(CONTR // 2)]
        for b in range(beads):
            at = b * CONTR + CONTR // 2
            total = own_ref[b, r : r + size, :]
            for j in range(CONTR // 2):
                total += parts[j] * table[at + j : at + j + 1]
            work_ref[b * stride + r : b * stride + r + size, :] = total
        for i in range(r, r + size):
            x, t = divmod(i, tiles)
            out_ref[x, :, t * LANES : (t + 1) * LANES] = work_ref[
                pl.ds(i, beads, stride=stride), :
            ]
        while done < 3 and (done + 1) * tiles <= r + size:
            moves.append(pltpu.make_async_copy(out_ref.at[done], out_to.at[done], sems.at[done]))
            moves[-1].start()
            done += 1
    for move in moves:
        move.wait()


VMEM = pl.BlockSpec(memory_space=pltpu.VMEM)
HBM = pl.BlockSpec(memory_space=pltpu.HBM)
PARAMS = pltpu.CompilerParams(vmem_limit_bytes=24 * 1024 * 1024)


FIRST = {"spots": 5, "factors": 5, "forces": 5}


def flipped(chip):
    return lax.div(chip, 4) if isinstance(chip, jax.Array) else chip // 4


def between(array, key):
    count = 8
    groups = []
    for side in range(2):
        for index in range(count):
            group = []
            for place in range(count):
                chip, block = place ^ FIRST[key], index
                if key == "factors":
                    chip, block = block, chip
                core = side ^ flipped(chip)
                group.append((2 * chip + core) * count + block)
            groups.append(group)
    return lax.all_to_all(
        array, ("bead", "atom"), 0, 0, axis_index_groups=groups, tiled=True
    )


def between_cores(array):
    peers = lax.axis_size("bead")
    return lax.ppermute(array, "bead", [(i, i ^ 1) for i in range(peers)])


def shaped(*shape, dtype=jnp.float32):
    return jax.ShapeDtypeStruct(shape, dtype)


def local(points, waves, labels, species):
    beads, _, sites = points.shape
    bead_peers = lax.axis_size("bead")
    atom_peers = lax.axis_size("atom")
    tiles = sites // LANES
    used = 3 * tiles
    rows = -(-(used + 3) // 8) * 8
    sent = -(-(used + 6) // 8) * 8
    held = -(-used // 8) * 8
    half = CONTR // 2
    chips = bead_peers // 2
    beads_all = beads * bead_peers
    work, given, charge, table = pl.pallas_call(
        functools.partial(contract_kernel, beads_all),
        out_shape=[
            shaped(rows * CONTR, LANES),
            shaped(half, rows, LANES),
            shaped(tiles, LANES),
            shaped(beads * CONTR, LANES),
        ],
        in_specs=[HBM] * 4,
        out_specs=[VMEM] * 4,
        scratch_shapes=[
            pltpu.VMEM((3, beads, sites), jnp.float32),
            pltpu.VMEM(waves.shape, jnp.int32),
            pltpu.VMEM((tiles, LANES), jnp.int32),
            pltpu.VMEM((1, species.shape[0]), jnp.float32),
            pltpu.SemaphoreType.DMA((6,)),
        ],
        compiler_params=PARAMS,
        name="contract",
    )(
        *(
            pltpu.with_memory_space_constraint(a, pltpu.HBM)
            for a in (
                points.transpose(1, 0, 2),
                waves,
                labels.reshape(tiles, LANES),
                species[None, :],
            )
        )
    )
    portion = pl.pallas_call(
        functools.partial(pair_sum_kernel, used),
        out_shape=shaped(chips, sent, LANES),
        in_specs=[VMEM] * 3,
        out_specs=VMEM,
        compiler_params=PARAMS,
        name="pair_sum",
    )(work, given, between_cores(given))
    spots = between(portion, "spots")
    partial, weights, high, low, plain = pl.pallas_call(
        functools.partial(structure_kernel, float(sites * atom_peers)),
        out_shape=[
            shaped(atom_peers, 2 * SENT, 2 * LANES),
            shaped(2 * ROWS, LANES),
            shaped(2 * LANES, sites, dtype=jnp.bfloat16),
            shaped(2 * LANES, sites, dtype=jnp.bfloat16),
            shaped(2 * ROWS, sites),
        ],
        in_specs=[VMEM] * 2,
        out_specs=[VMEM] * 5,
        scratch_shapes=[pltpu.VMEM((4 * ROWS, sites), jnp.bfloat16)],
        compiler_params=PARAMS,
        name="structure",
    )(spots, charge)
    factors = between(partial, "factors")
    force = pl.pallas_call(
        force_kernel,
        out_shape=shaped(chips, held, LANES),
        in_specs=[VMEM] * 5,
        out_specs=VMEM,
        scratch_shapes=[
            pltpu.VMEM((6 * ROWS, 2 * LANES), jnp.float32),
            pltpu.VMEM((used, LANES), jnp.float32),
        ],
        compiler_params=PARAMS,
        name="force",
    )(factors, weights, high, low, plain)
    gathered = pl.pallas_call(
        functools.partial(gather_kernel, used),
        out_shape=shaped(half, held, LANES),
        in_specs=[VMEM],
        out_specs=VMEM,
        compiler_params=PARAMS,
        name="gather",
    )(between(force, "forces"))
    taken = between_cores(gathered)
    own = pl.pallas_call(
        functools.partial(own_kernel, used),
        out_shape=shaped(beads, held, LANES),
        in_specs=[VMEM] * 2,
        out_specs=VMEM,
        compiler_params=PARAMS,
        cost_estimate=pl.CostEstimate(flops=300000, bytes_accessed=300000, transcendentals=0),
        name="own",
    )(table, gathered)
    out = pl.pallas_call(
        expand_kernel,
        out_shape=shaped(3, beads, sites),
        in_specs=[VMEM] * 3,
        out_specs=HBM,
        scratch_shapes=[
            pltpu.VMEM((beads * held, LANES), jnp.float32),
            pltpu.VMEM((3, beads, sites), jnp.float32),
            pltpu.SemaphoreType.DMA((3,)),
        ],
        compiler_params=PARAMS,
        name="expand",
    )(table, own, taken)
    return out.transpose(1, 0, 2)


def solution(mesh):
    in_specs = (P("bead", None, "atom"), P(None, "bead"), P("atom"), P())
    out_specs = P("bead", None, "atom")
    return jax.shard_map(local, mesh=mesh, in_specs=in_specs, out_specs=out_specs, check_vma=False)
```

```python
import functools
import math

import jax
import jax.numpy as jnp
import numpy as np
from jax import lax
from jax.experimental import pallas as pl
from jax.experimental.pallas import tpu as pltpu
from jax.sharding import PartitionSpec as P

CONTR = 8
LANES = 128
ROWS = 16
SENT = 12
TWO_PI = 2.0 * math.pi


def polynomials():
    nodes = 0.5 * np.cos(np.pi * (np.arange(400) + 0.5) / 400)
    u = nodes * nodes
    odd = np.linalg.lstsq(
        nodes[:, None] * u[:, None] ** np.arange(6), np.sin(2 * np.pi * nodes), rcond=None
    )[0]
    even = np.linalg.lstsq(u[:, None] ** np.arange(7), np.cos(2 * np.pi * nodes), rcond=None)[0]
    return [float(c) for c in odd], [float(c) for c in even]


ODD, EVEN = polynomials()


def horner(u, coefficients):
    total = coefficients[-1]
    for c in coefficients[-2::-1]:
        total = total * u + c
    return total


def reduced(t):
    return t - jnp.round(t)


def sin_turns(t):
    t = reduced(t)
    return t * horner(t * t, ODD)


def cos_turns(t):
    t = reduced(t)
    return horner(t * t, EVEN)


def both_turns(t):
    t = reduced(t)
    u = t * t
    return horner(u, EVEN), t * horner(u, ODD)


def iota(shape, dim):
    return lax.broadcasted_iota(jnp.int32, shape, dim).astype(jnp.float32)


def pair_of(index, core):
    tile = jnp.floor(index * 0.125)
    place = index - 8.0 * tile
    run = jnp.floor((tile + 0.5) * 0.2)
    m2 = tile - 5.0 * run + 1.0 + 5.0 * core
    last = run > 2.5
    m2 = jnp.where(last, 0.0, m2)
    run = jnp.where(last, core, run)
    return m2, run_member(run, place)


def run_member(run, place):
    middle = jnp.where(place < 0.5, 0.0, jnp.where(place < 2.5, place + 8.0, -6.0 - place))
    return jnp.where(run < 0.5, place + 1.0, jnp.where(run < 1.5, middle, -1.0 - place))


def place_of(m2, m3, core):
    size = jnp.abs(m3)
    middle = (size > 8.5) | (size < 0.5)
    run = jnp.where(middle, 1.0, jnp.where(m3 < 0, 2.0, 0.0))
    inner = jnp.where(m3 < 0, size - 6.0, jnp.maximum(size - 8.0, 0.0))
    place = jnp.where(middle, inner, size - 1.0)
    step = m2 - 1.0 - 5.0 * core
    row = (run * 5.0 + step) * 8.0 + place
    row = jnp.where((step >= 0) & (step < 5), row, -1.0)
    return jnp.where(m2 == 0.0, jnp.where(run == core, 120.0 + place, -1.0), row)


def split(value):
    high = value.astype(jnp.bfloat16)
    low = (value - high.astype(jnp.float32)).astype(jnp.bfloat16)
    return high, low


def dot_nt(a, b):
    return lax.dot_general(a, b, (((1,), (1,)), ((), ())), preferred_element_type=jnp.float32)


def table_value(bead, contracted, beads):
    turn = bead * (1.0 / beads) - contracted * (1.0 / CONTR)
    total = 1.0 + math.sqrt(2.0) * cos_turns(turn * (CONTR // 2))
    for mode in range(1, CONTR // 2):
        total += 2.0 * cos_turns(turn * mode)
    return total * (1.0 / beads)


def contract_kernel(
    beads_all,
    points_from,
    waves_from,
    labels_from,
    species_from,
    work_ref,
    given_ref,
    charge_ref,
    table_ref,
    points_ref,
    waves_ref,
    labels_ref,
    species_ref,
    sems,
):
    copies_in = [
        pltpu.make_async_copy(points_from.at[x], points_ref.at[x], sems.at[x]) for x in range(3)
    ]
    for i, (source, target) in enumerate(
        ((waves_from, waves_ref), (labels_from, labels_ref), (species_from, species_ref))
    ):
        copies_in.append(pltpu.make_async_copy(source, target, sems.at[3 + i]))
    for copy in copies_in:
        copy.start()
    beads = points_ref.shape[1]
    tiles = points_ref.shape[2] // LANES
    bead_index = lax.axis_index("bead")
    first = (bead_index * beads).astype(jnp.float32)
    flip = flipped(lax.div(bead_index, 2))
    start = (lax.rem(bead_index + flip, 2) * (CONTR // 2)).astype(jnp.float32)
    columns = [
        table_value(first + b, iota((CONTR, LANES), 0) + start, beads_all) for b in range(beads)
    ]
    for b in range(beads):
        table_ref[b * CONTR : (b + 1) * CONTR, :] = columns[b]
    for x in range(3):
        copies_in[x].wait()
        for t in range(tiles):
            block = points_ref[x, :, t * LANES : (t + 1) * LANES]
            total = columns[0] * jnp.broadcast_to(block[0:1], (CONTR, LANES))
            for b in range(1, beads):
                total += columns[b] * jnp.broadcast_to(block[b : b + 1], (CONTR, LANES))
            row = (x * tiles + t) * CONTR
            work_ref[row : row + CONTR, :] = total
    used = 3 * tiles
    half = CONTR // 2
    for j in range(half):
        given_ref[j, 0:used, :] = work_ref[pl.ds(half + j, used, stride=CONTR), :]
    for copy in copies_in[3:]:
        copy.wait()
    waves = waves_ref[...].astype(jnp.float32)
    given_ref[0, used : used + 3, :] = waves
    labels = labels_ref[...]
    charge = jnp.zeros(labels.shape, jnp.float32)
    for kind in range(species_ref.shape[1]):
        value = jnp.broadcast_to(species_ref[:, kind : kind + 1], labels.shape)
        charge += jnp.where(labels == kind, value, 0.0)
    charge_ref[...] = charge


def pair_sum_kernel(used, work_ref, given_ref, taken_ref, out_ref):
    copies = out_ref.shape[0] // given_ref.shape[0]
    kept_waves = given_ref[0, used : used + 3, :]
    taken_waves = taken_ref[0, used : used + 3, :]
    for j in range(given_ref.shape[0]):
        total = work_ref[pl.ds(j, used, stride=CONTR), :] + taken_ref[j, 0:used, :]
        for c in range(copies):
            out_ref[j * copies + c, 0:used, :] = total
            out_ref[j * copies + c, used : used + 3, :] = kept_waves
            out_ref[j * copies + c, used + 3 : used + 6, :] = taken_waves


def members(key):
    return [place ^ FIRST[key] for place in range(8)]


def own_half():
    first = FIRST["spots"]
    bit = lax.rem(lax.div(lax.axis_index("bead"), 2) + first % 2, 2)
    return bit.astype(jnp.float32)


def structure_kernel(
    number_points,
    spots_ref,
    charge_ref,
    partial_ref,
    weights_ref,
    high_ref,
    low_ref,
    plain_ref,
    charged_ref,
):
    half = own_half()
    peers = spots_ref.shape[0]
    tiles = charge_ref.shape[0]
    used = 3 * tiles
    spots = spots_ref[0, 0:used, :]
    for p in range(1, peers):
        spots += spots_ref[p, 0:used, :]
    spots = reduced(spots)
    charge = charge_ref[...]
    grid_row = iota((2 * ROWS, LANES), 0)
    back = grid_row >= ROWS
    size = jnp.where(back, grid_row - ROWS, grid_row)
    wanted = jnp.where(back, jnp.where(size > 0, -size, 1000.0), size)
    pair_row = iota((LANES, LANES), 0).astype(jnp.bfloat16)
    wanted = wanted.astype(jnp.bfloat16)
    one, zero = jnp.bfloat16(1.0), jnp.bfloat16(0.0)
    m1, m2, m3 = (
        jnp.concatenate([spots_ref[:, used + x, :], spots_ref[:, used + 3 + x, :]], axis=0)
        for x in range(3)
    )
    sign = jnp.where(m2 < 0, -1.0, 1.0)
    sign = jnp.where((m2 == 0) & (m3 < 0), -1.0, sign)
    m1 = (m1 * sign).astype(jnp.bfloat16)
    place = place_of(m2 * sign, m3 * sign, half).astype(jnp.bfloat16)
    counts = jnp.zeros((2 * ROWS, LANES), jnp.float32)
    for p in range(2 * peers):
        left = jnp.where(wanted == m1[p : p + 1], one, zero)
        right = jnp.where(pair_row == place[p : p + 1], one, zero)
        counts += dot_nt(left, right)
    m2, m3 = pair_of(iota((2 * ROWS, LANES), 1), half)
    square = size * size + m2 * m2 + m3 * m3
    square = jnp.maximum(square, 1.0)
    weights_ref[...] = counts * (4.0 * jnp.exp(square * -0.01) / (square * number_points))
    size = iota((ROWS, LANES), 0)
    steps = 1.0 + 5.0 * half + iota((8, LANES), 0)
    place = iota((8, LANES), 0)
    outer, middle = (run_member(jnp.full((8, LANES), run), place) for run in (0.0, 1.0))
    for t in range(tiles):
        lanes = slice(t * LANES, (t + 1) * LANES)
        x1 = spots[t : t + 1, :]
        x2 = spots[tiles + t : tiles + t + 1, :]
        x3 = spots[2 * tiles + t : 2 * tiles + t + 1, :]
        q = charge[t : t + 1, :]
        for index, value in enumerate(both_turns(size * x1)):
            value = q * value
            at = index * ROWS
            plain_ref[index * SENT : (index + 1) * SENT, lanes] = value[0:SENT]
            high, low = split(value)
            charged_ref[at : at + ROWS, lanes] = high
            charged_ref[2 * ROWS + at : 3 * ROWS + at, lanes] = low
        cos2, sin2 = both_turns(steps * x2)
        cos3, sin3 = both_turns(outer * x3)
        cos4, sin4 = both_turns(middle * x3)
        cosines, sines = [None] * 15, [None] * 15
        for i in range(5):
            c2 = jnp.broadcast_to(cos2[i : i + 1], (8, LANES))
            s2 = jnp.broadcast_to(sin2[i : i + 1], (8, LANES))
            cc, ss, sc, cs = c2 * cos3, s2 * sin3, s2 * cos3, c2 * sin3
            cosines[i], sines[i] = cc - ss, sc + cs
            cosines[5 + i], sines[5 + i] = c2 * cos4 - s2 * sin4, s2 * cos4 + c2 * sin4
            cosines[10 + i], sines[10 + i] = cc + ss, sc - cs
        cosines.append(jnp.where(half == 0.0, cos3, cos4))
        sines.append(jnp.where(half == 0.0, sin3, sin4))
        for index, values in enumerate((cosines, sines)):
            for r in range(0, 16, 2):
                high, low = split(jnp.concatenate(values[r : r + 2], axis=0))
                at = index * LANES + r * 8
                high_ref[at : at + 16, lanes] = high
                low_ref[at : at + 16, lanes] = low
    total = dot_nt(charged_ref[...], high_ref[...])
    total = (
        total[0 : 2 * ROWS]
        + total[2 * ROWS :]
        + dot_nt(charged_ref[0 : 2 * ROWS, :], low_ref[...])
    )
    for p in range(partial_ref.shape[0]):
        partial_ref[p, 0:SENT, :] = total[0:SENT]
        partial_ref[p, SENT:, :] = total[ROWS : ROWS + SENT]


def force_kernel(
    partial_ref, weights_ref, high_ref, low_ref, plain_ref, out_ref, coef_ref, term_ref
):
    half = own_half()
    tiles = plain_ref.shape[1] // LANES
    cos_row = partial_ref[0, 0:SENT, :]
    sin_row = partial_ref[0, SENT:, :]
    for p in range(1, partial_ref.shape[0]):
        cos_row += partial_ref[p, 0:SENT, :]
        sin_row += partial_ref[p, SENT:, :]
    ahead = weights_ref[0:SENT, :]
    back = weights_ref[ROWS : ROWS + SENT, :]
    cc, cs = cos_row[:, :LANES], cos_row[:, LANES:]
    sc, ss = sin_row[:, :LANES], sin_row[:, LANES:]
    ahead_cos, ahead_sin = ahead * (cc - ss), ahead * (cs + sc)
    back_cos, back_sin = back * (cc + ss), back * (cs - sc)
    m2, m3 = pair_of(iota((SENT, LANES), 1), half)
    coef_ref[...] = jnp.zeros_like(coef_ref)
    rows = (
        (ahead_cos + back_cos, ahead_sin + back_sin),
        (ahead_sin - back_sin, back_cos - ahead_cos),
    )
    m1 = TWO_PI * iota((SENT, LANES), 0)
    for kind, (on_cos, on_sin) in enumerate(rows):
        at = (1 - kind) * SENT
        along = m1 if kind == 0 else -m1
        coef_ref[at : at + SENT, :LANES] = along * on_cos
        coef_ref[at : at + SENT, LANES:] = along * on_sin
        for axis, m in enumerate((m2, m3)):
            at = kind * SENT + 2 * SENT * (axis + 1)
            coef_ref[at : at + SENT, :LANES] = (-TWO_PI) * m * on_sin
            coef_ref[at : at + SENT, LANES:] = TWO_PI * m * on_cos
    high, low = split(coef_ref[...])
    both = jnp.concatenate([high, low], axis=0)
    size = high.shape[0]
    width = 2 * LANES
    for t in range(0, tiles, 2):
        lanes = slice(t * LANES, t * LANES + width)
        near = jnp.dot(both, high_ref[:, lanes], preferred_element_type=jnp.float32)
        far = jnp.dot(high, low_ref[:, lanes], preferred_element_type=jnp.float32)
        term = near[:size] + near[size:] + far
        plain = plain_ref[:, lanes]
        for x in range(3):
            at = 2 * SENT * x
            total = jnp.sum(term[at : at + 2 * SENT] * plain, axis=0, keepdims=True)
            for i in range(2):
                term_ref[x * tiles + t + i : x * tiles + t + i + 1, :] = total[
                    :, i * LANES : (i + 1) * LANES
                ]
    block = term_ref[...]
    for p in range(out_ref.shape[0]):
        out_ref[p, 0 : block.shape[0], :] = block


def gather_kernel(used, force_ref, out_ref):
    arrivals = members("forces")
    senders = [arrivals.index(member) for member in members("spots")]
    copies = force_ref.shape[0] // out_ref.shape[0]
    for j in range(out_ref.shape[0]):
        total = force_ref[senders[j * copies], 0:used, :]
        for c in range(1, copies):
            total += force_ref[senders[j * copies + c], 0:used, :]
        out_ref[j, 0:used, :] = total


def own_kernel(used, table_ref, kept_ref, out_ref):
    parts = [kept_ref[j, 0:used, :] for j in range(kept_ref.shape[0])]
    for b in range(out_ref.shape[0]):
        at = b * CONTR
        total = parts[0] * table_ref[at : at + 1]
        for j in range(1, len(parts)):
            total += parts[j] * table_ref[at + j : at + j + 1]
        out_ref[b, 0:used, :] = total


def expand_kernel(table_ref, own_ref, taken_ref, out_to, work_ref, out_ref, sems):
    beads = out_ref.shape[1]
    tiles = out_ref.shape[2] // LANES
    used = 3 * tiles
    stride = work_ref.shape[0] // beads
    table = table_ref[...]
    done = 0
    moves = []
    for r in range(0, used, 8):
        size = min(8, used - r)
        parts = [taken_ref[j, r : r + size, :] for j in range(CONTR // 2)]
        for b in range(beads):
            at = b * CONTR + CONTR // 2
            total = own_ref[b, r : r + size, :]
            for j in range(CONTR // 2):
                total += parts[j] * table[at + j : at + j + 1]
            work_ref[b * stride + r : b * stride + r + size, :] = total
        for i in range(r, r + size):
            x, t = divmod(i, tiles)
            out_ref[x, :, t * LANES : (t + 1) * LANES] = work_ref[
                pl.ds(i, beads, stride=stride), :
            ]
        while done < 3 and (done + 1) * tiles <= r + size:
            moves.append(pltpu.make_async_copy(out_ref.at[done], out_to.at[done], sems.at[done]))
            moves[-1].start()
            done += 1
    for move in moves:
        move.wait()


VMEM = pl.BlockSpec(memory_space=pltpu.VMEM)
HBM = pl.BlockSpec(memory_space=pltpu.HBM)
PARAMS = pltpu.CompilerParams(vmem_limit_bytes=24 * 1024 * 1024)


FIRST = {"spots": 5, "factors": 5, "forces": 5}


def flipped(chip):
    return lax.div(chip, 4) if isinstance(chip, jax.Array) else chip // 4


def between(array, key):
    count = 8
    groups = []
    for side in range(2):
        for index in range(count):
            group = []
            for place in range(count):
                chip, block = place ^ FIRST[key], index
                if key == "factors":
                    chip, block = block, chip
                core = side ^ flipped(chip)
                group.append((2 * chip + core) * count + block)
            groups.append(group)
    return lax.all_to_all(
        array, ("bead", "atom"), 0, 0, axis_index_groups=groups, tiled=True
    )


def between_cores(array):
    peers = lax.axis_size("bead")
    return lax.ppermute(array, "bead", [(i, i ^ 1) for i in range(peers)])


def shaped(*shape, dtype=jnp.float32):
    return jax.ShapeDtypeStruct(shape, dtype)


def local(points, waves, labels, species):
    beads, _, sites = points.shape
    bead_peers = lax.axis_size("bead")
    atom_peers = lax.axis_size("atom")
    tiles = sites // LANES
    used = 3 * tiles
    rows = -(-(used + 3) // 8) * 8
    sent = -(-(used + 6) // 8) * 8
    held = -(-used // 8) * 8
    half = CONTR // 2
    chips = bead_peers // 2
    beads_all = beads * bead_peers
    work, given, charge, table = pl.pallas_call(
        functools.partial(contract_kernel, beads_all),
        out_shape=[
            shaped(rows * CONTR, LANES),
            shaped(half, rows, LANES),
            shaped(tiles, LANES),
            shaped(beads * CONTR, LANES),
        ],
        in_specs=[HBM] * 4,
        out_specs=[VMEM] * 4,
        scratch_shapes=[
            pltpu.VMEM((3, beads, sites), jnp.float32),
            pltpu.VMEM(waves.shape, jnp.int32),
            pltpu.VMEM((tiles, LANES), jnp.int32),
            pltpu.VMEM((1, species.shape[0]), jnp.float32),
            pltpu.SemaphoreType.DMA((6,)),
        ],
        compiler_params=PARAMS,
        name="contract",
    )(
        *(
            pltpu.with_memory_space_constraint(a, pltpu.HBM)
            for a in (
                points.transpose(1, 0, 2),
                waves,
                labels.reshape(tiles, LANES),
                species[None, :],
            )
        )
    )
    portion = pl.pallas_call(
        functools.partial(pair_sum_kernel, used),
        out_shape=shaped(chips, sent, LANES),
        in_specs=[VMEM] * 3,
        out_specs=VMEM,
        compiler_params=PARAMS,
        name="pair_sum",
    )(work, given, between_cores(given))
    spots = between(portion, "spots")
    partial, weights, high, low, plain = pl.pallas_call(
        functools.partial(structure_kernel, float(sites * atom_peers)),
        out_shape=[
            shaped(atom_peers, 2 * SENT, 2 * LANES),
            shaped(2 * ROWS, LANES),
            shaped(2 * LANES, sites, dtype=jnp.bfloat16),
            shaped(2 * LANES, sites, dtype=jnp.bfloat16),
            shaped(2 * SENT, sites),
        ],
        in_specs=[VMEM] * 2,
        out_specs=[VMEM] * 5,
        scratch_shapes=[pltpu.VMEM((4 * ROWS, sites), jnp.bfloat16)],
        compiler_params=PARAMS,
        name="structure",
    )(spots, charge)
    factors = between(partial, "factors")
    force = pl.pallas_call(
        force_kernel,
        out_shape=shaped(chips, held, LANES),
        in_specs=[VMEM] * 5,
        out_specs=VMEM,
        scratch_shapes=[
            pltpu.VMEM((-(-6 * SENT // 16) * 16, 2 * LANES), jnp.float32),
            pltpu.VMEM((used, LANES), jnp.float32),
        ],
        compiler_params=PARAMS,
        name="force",
    )(factors, weights, high, low, plain)
    gathered = pl.pallas_call(
        functools.partial(gather_kernel, used),
        out_shape=shaped(half, held, LANES),
        in_specs=[VMEM],
        out_specs=VMEM,
        compiler_params=PARAMS,
        name="gather",
    )(between(force, "forces"))
    taken = between_cores(gathered)
    own = pl.pallas_call(
        functools.partial(own_kernel, used),
        out_shape=shaped(beads, held, LANES),
        in_specs=[VMEM] * 2,
        out_specs=VMEM,
        compiler_params=PARAMS,
        cost_estimate=pl.CostEstimate(flops=300000, bytes_accessed=300000, transcendentals=0),
        name="own",
    )(table, gathered)
    out = pl.pallas_call(
        expand_kernel,
        out_shape=shaped(3, beads, sites),
        in_specs=[VMEM] * 3,
        out_specs=HBM,
        scratch_shapes=[
            pltpu.VMEM((beads * held, LANES), jnp.float32),
            pltpu.VMEM((3, beads, sites), jnp.float32),
            pltpu.SemaphoreType.DMA((3,)),
        ],
        compiler_params=PARAMS,
        name="expand",
    )(table, own, taken)
    return out.transpose(1, 0, 2)


def solution(mesh):
    in_specs = (P("bead", None, "atom"), P(None, "bead"), P("atom"), P())
    out_specs = P("bead", None, "atom")
    return jax.shard_map(local, mesh=mesh, in_specs=in_specs, out_specs=out_specs, check_vma=False)
```
